256 devices in a mesh: ctx: 32 (over y, x, core), ch: 8 (over z).
Axes of the slice: x: 4, y: 4, z: 8, core: 2. Of those that a mesh axis runs over, the one named last changes fastest.
Arguments:
- hidden: bfloat16 [8192, 32768], P('ch', 'ctx'), may hold values from -24 to 24
- cotangent: bfloat16 [8192, 32768], P('ch', 'ctx'), may hold values from -24 to 24
- norm_gain: float32 [8192], P('ch'), may hold values from 0.5 to 1.5
- mr_filter: bfloat16 [512, 128], P('ch'), may hold values from -0.5 to 0.5
- residue: float32 [512, 16], P('ch'), may hold values from -1.5 to 1.5
- decay_rate: float32 [512, 16], P('ch'), may hold values from 4.7683716e-07 to 0.033
- skip_weight: float32 [8192], P('ch'), may hold values from -3 to 3
Outputs:
- grad_hidden: bfloat16 [8192, 32768], P('ch', 'ctx')
- grad_gain: float32 [8192], P('ch')
- grad_mr: float32 [512, 128], P('ch')
- grad_residue: float32 [512, 16], P('ch')
- grad_log_rate: float32 [512, 16], P('ch')
- grad_skip: float32 [8192], P('ch')
- grad_inv_rms: float32 [32768], P('ctx')
The draws below stay inside these ranges and needn't reach their ends.
All inputs are finite; a program needn't handle non-finite values.
Results may differ from the reference program's by a relative error of at most 0.005.
Values may be sent and summed in bfloat16 or wider, within the bound.
No kernel may reach another device: no remote copies, remote signals or barrier semaphores. Data moves between devices by JAX's collectives and lax.ppermute only.
A program may use at most 192 MiB of HBM per device.

```python
import math
import jax
import jax.numpy as jnp
from jax import lax

D = 8192
GROUP = 16
TAPS = 128
MODES = 16
GROUPS = 512
SEQ = 32768


def draw_hidden(key, part):
    first_key, second_key = jax.random.split(key, 2)
    values = jax.random.normal(first_key, (D, SEQ), jnp.float32)
    channel_pos = jnp.arange(D).astype(jnp.float32) / D
    roughness = jax.random.uniform(second_key, (D, 1), jnp.float32, 0.6, 1.4)
    scales = jnp.exp(jnp.log(3.0) * channel_pos)[:, None] * roughness
    return jnp.clip(values * scales, -24.0, 24.0).astype(jnp.bfloat16)


def draw_cotangent(key, part):
    first_key, second_key = jax.random.split(key, 2)
    values = jax.random.normal(first_key, (D, SEQ), jnp.float32)
    token_pos = jnp.arange(SEQ).astype(jnp.float32) / SEQ
    roughness = jax.random.uniform(second_key, (1, SEQ), jnp.float32, 0.6, 1.4)
    scales = jnp.exp(jnp.log(3.0) * token_pos)[None, :] * roughness
    return jnp.clip(values * scales, -24.0, 24.0).astype(jnp.bfloat16)


def steps_of(rng, shape, cuts, low, high):
    factor_of = 1.0
    for axis_at, shards_of in cuts:
        steps = jax.random.uniform(jax.random.fold_in(jax.random.fold_in(rng, 6), axis_at), (shards_of,), jnp.float32, low / len(cuts), high / len(cuts))
        factor_of = factor_of * jnp.repeat(jnp.exp(steps), shape[axis_at] // shards_of).reshape((-1,) + (1,) * (len(shape) - 1 - axis_at))
    return factor_of


def scatter_about(rng, dims, deviation, reach, cuts=(), kind=jnp.bfloat16):
    entries = jax.random.normal(rng, dims, jnp.float32) * deviation
    if len(cuts) > 0:
        entries = steps_of(rng, dims, cuts, -0.22, 0.18) * entries
    return jnp.clip(entries, min=-reach, max=reach).astype(kind)


def setup_inputs(seed: int = 0) -> dict:
    key_list = jax.random.split(jax.random.key(seed), 8)
    hidden = draw_hidden(jax.random.fold_in(key_list[7], 71), 0)
    cotangent = draw_cotangent(jax.random.fold_in(key_list[7], 71), 0)
    norm_gain = jnp.clip(1.0 + 0.1 * jax.random.normal(key_list[2], (D,), jnp.float32), 0.5, 1.5)
    mr_filter = scatter_about(key_list[3], (GROUPS, TAPS), TAPS ** -0.5, 0.5, ((0, 8),))
    residue = scatter_about(key_list[4], (GROUPS, MODES), 0.25, 1.5, ((0, 8),), jnp.float32)
    decay_rate = jnp.clip(jnp.exp(math.log(0.033) - 11.144843 * jax.random.uniform(key_list[5], (GROUPS, MODES), jnp.float32) ** steps_of(key_list[5], (GROUPS, MODES), ((0, 8),), -0.2, 0.2)), 4.76837158203125e-07, 0.033)
    skip_weight = scatter_about(key_list[6], (D,), 0.5, 3.0, ((0, 8),), jnp.float32)
    return dict(hidden=hidden, cotangent=cotangent, norm_gain=norm_gain, mr_filter=mr_filter, residue=residue, decay_rate=decay_rate, skip_weight=skip_weight)


eps_norm = 1e-06
top_precision = lax.Precision.HIGHEST

def reference(hidden, cotangent, norm_gain, mr_filter, residue, decay_rate, skip_weight):
    block_width = 16 * GROUP
    block_total = D // block_width
    group_count = block_width // GROUP
    grad_scale = SEQ ** (-0.5)
    fft_length = 2 * SEQ
    lag_values = jnp.arange(SEQ).astype(jnp.float32)

    def add_squares(running, block_index):
        hidden_rows = lax.dynamic_slice_in_dim(hidden, block_index * block_width, block_width, 0).astype(jnp.float32)
        return (running + lax.optimization_barrier(jnp.sum(hidden_rows * hidden_rows, axis=0)), None)
    squares, _ignored = lax.scan(add_squares, jnp.zeros((SEQ,), jnp.float32), jnp.arange(block_total))
    inverse_rms = lax.rsqrt(squares / D + eps_norm)

    def one_block(dot_running, block_index):
        start = block_index * block_width
        group_start = block_index * group_count
        hidden_rows = lax.dynamic_slice_in_dim(hidden, start, block_width, 0).astype(jnp.float32)
        grad_rows = lax.dynamic_slice_in_dim(cotangent, start, block_width, 0).astype(jnp.float32)
        gains = lax.dynamic_slice_in_dim(norm_gain, start, block_width, 0)
        skips = lax.dynamic_slice_in_dim(skip_weight, start, block_width, 0)
        short_taps = lax.dynamic_slice_in_dim(mr_filter, group_start, group_count, 0).astype(jnp.float32)
        residues = lax.dynamic_slice_in_dim(residue, group_start, group_count, 0)
        rates = lax.dynamic_slice_in_dim(decay_rate, group_start, group_count, 0)
        normed = hidden_rows * inverse_rms[None, :]
        normal_unit = lax.optimization_barrier((normed * gains[:, None]).astype(jnp.bfloat16)).astype(jnp.float32)
        channel_taps = jnp.repeat(short_taps, GROUP, axis=0)
        padded = jnp.pad(normal_unit, ((0, 0), (TAPS - 1, 0)))

        def forward_tap(tap_index, running):
            piece = lax.dynamic_slice_in_dim(padded, TAPS - 1 - tap_index, SEQ, 1)
            weight_col = lax.dynamic_slice_in_dim(channel_taps, tap_index, 1, 1)
            return running + weight_col * piece
        mixed = lax.fori_loop(0, TAPS, forward_tap, jnp.zeros((block_width, SEQ), jnp.float32))
        mixed = lax.optimization_barrier(mixed.astype(jnp.bfloat16)).astype(jnp.float32)
        amplitude = residues * jnp.sqrt(2.0 * rates)
        powers = jnp.exp(-rates[:, :, None] * lag_values[None, None, :])
        long_kernel = jnp.einsum('gn,gnt->gt', amplitude, powers, precision=top_precision)
        kernel_freq = jnp.repeat(jnp.fft.rfft(long_kernel, fft_length, axis=1), GROUP, axis=0)
        reversed_grad = jnp.fft.rfft(grad_rows[:, ::-1], fft_length, axis=1)
        correlated = jnp.fft.irfft(kernel_freq * reversed_grad, fft_length, axis=1)[:, :SEQ][:, ::-1]
        grad_mixed = lax.optimization_barrier((correlated + skips[:, None] * grad_rows).astype(jnp.bfloat16)).astype(jnp.float32)
        skip_grad = lax.optimization_barrier(jnp.sum(grad_rows * mixed, axis=1)) * grad_scale
        cross_freq = jnp.fft.rfft(grad_rows, fft_length, axis=1) * jnp.fft.rfft(mixed[:, ::-1], fft_length, axis=1)
        cross_freq = lax.optimization_barrier(jnp.sum(cross_freq.reshape(group_count, GROUP, -1), axis=1))
        lag_corr = jnp.fft.irfft(cross_freq, fft_length, axis=1)[:, SEQ - 1:2 * SEQ - 1]
        first_moment = jnp.einsum('gt,gnt->gn', lag_corr, powers, precision=top_precision)
        second_moment = jnp.einsum('gt,gnt->gn', lag_corr * lag_values[None, :], powers, precision=top_precision)
        residue_grad = jnp.sqrt(2.0 * rates) * first_moment * grad_scale
        rate_grad = amplitude * (0.5 * first_moment - rates * second_moment) * grad_scale
        grad_padded = jnp.pad(grad_mixed, ((0, 0), (0, TAPS - 1)))

        def backward_tap(tap_index, carried):
            running, tap_terms = carried
            ahead = lax.dynamic_slice_in_dim(grad_padded, tap_index, SEQ, 1)
            weight_col = lax.dynamic_slice_in_dim(channel_taps, tap_index, 1, 1)
            behind = lax.dynamic_slice_in_dim(padded, TAPS - 1 - tap_index, SEQ, 1)
            term = lax.optimization_barrier(jnp.sum(grad_mixed * behind, axis=1))
            tap_terms = lax.dynamic_update_slice_in_dim(tap_terms, term[:, None], tap_index, 1)
            return (running + weight_col * ahead, tap_terms)
        input_grad, tap_terms = lax.fori_loop(0, TAPS, backward_tap, (jnp.zeros((block_width, SEQ), jnp.float32), jnp.zeros((block_width, TAPS), jnp.float32)))
        short_grad = lax.optimization_barrier(jnp.sum(tap_terms.reshape(group_count, GROUP, TAPS), axis=1)) * grad_scale
        pulled = input_grad * gains[:, None]
        gain_grad = lax.optimization_barrier(jnp.sum(input_grad * normed, axis=1)) * grad_scale
        dot_running = dot_running + lax.optimization_barrier(jnp.sum(pulled * normed, axis=0))
        return (dot_running, (pulled, gain_grad, short_grad, residue_grad, rate_grad, skip_grad))
    row_dot, results = lax.scan(one_block, jnp.zeros((SEQ,), jnp.float32), jnp.arange(block_total))
    pulled_all, gain_all, short_all, residue_all, rate_all, skip_all = results
    grad_inv_rms = row_dot / inverse_rms * D ** (-0.5)

    def finish_block(pieces):
        block_index, pulled = pieces
        hidden_rows = lax.dynamic_slice_in_dim(hidden, block_index * block_width, block_width, 0).astype(jnp.float32)
        normed = hidden_rows * inverse_rms[None, :]
        return (inverse_rms[None, :] * (pulled - normed * row_dot[None, :] / D)).astype(jnp.bfloat16)
    grad_hidden = lax.map(finish_block, (jnp.arange(block_total), pulled_all)).reshape(D, SEQ)
    return (grad_hidden, gain_all.reshape(D), short_all.reshape(GROUPS, TAPS), residue_all.reshape(GROUPS, MODES), rate_all.reshape(GROUPS, MODES), skip_all.reshape(D), grad_inv_rms)
```

```python
import functools

import jax
import jax.numpy as jnp
from jax import lax
from jax.experimental import pallas as pl
from jax.experimental.pallas import tpu as pltpu
from jax.sharding import PartitionSpec as P

eps_norm = 1e-06
B = 128
GB = 8
f32 = jnp.float32
bf16 = jnp.bfloat16

NN = (((1,), (0,)), ((), ()))
NT = (((1,), (1,)), ((), ()))
TN = (((0,), (0,)), ((), ()))


def mm(a, b, dims):
    return lax.dot_general(a, b, dims, preferred_element_type=f32)


def split(x):
    hi = x.astype(bf16)
    lo = (x - hi.astype(f32)).astype(bf16)
    return hi, lo


def iotas(shape):
    return (
        lax.broadcasted_iota(jnp.int32, shape, 0),
        lax.broadcasted_iota(jnp.int32, shape, 1),
    )


def toeplitz(row):
    full = jnp.broadcast_to(row, (B, B))
    return pltpu.roll(full, 0, 1, stride=1, stride_axis=0)


def lag_sums(square):
    total = square[:8]
    for a in range(8, B, 8):
        total = total + pltpu.roll(square[a : a + 8], B - a, 1)
    row = lax.broadcasted_iota(jnp.int32, (8, B), 0)
    for bit in (1, 2, 4):
        total = jnp.where((row & bit) != 0, pltpu.roll(total, B - bit, 1), total)
    return jnp.sum(total, axis=0, keepdims=True)


def grads_kernel(nb, ct_ref, ctn_ref, e0_ref, g_ref, k_ref, d_ref, skip_ref, gml_ref, aft_ref):
    row, lane = iotas((B, B))
    upper = lane >= row
    step_lane = lax.broadcasted_iota(jnp.int32, (16, B), 1)
    steps = step_lane.astype(f32)
    third = (step_lane >= 32) & (step_lane < 48)
    zeros = jnp.zeros((16, B), f32)
    for g in range(GB):
        rows = pl.ds(16 * g, 16)
        blocks = [ct_ref[rows, pl.ds(B * b, B)] for b in range(nb)] + [ctn_ref[rows, :]]
        lhs = jnp.concatenate(blocks, axis=0)
        toe = jnp.where(upper, toeplitz(k_ref[pl.ds(g, 1), :]), 0.0)
        e0 = e0_ref[g]
        weights = jnp.concatenate([toe, e0, e0 * steps, e0, e0, zeros, zeros, zeros, zeros], axis=0)
        hi, lo = split(weights)
        out = mm(jnp.concatenate([lhs, lhs], axis=1), jnp.concatenate([hi, lo], axis=1), NT)
        near = out[:, :B]
        states = out[:, B:]
        decay = jnp.broadcast_to(d_ref[pl.ds(g, 1), :], (16, B))
        after = zeros
        found = [after]
        for b in range(nb, 0, -1):
            state = states[16 * b : 16 * b + 16]
            state = jnp.where(third, state * float(B * b), state)
            after = state + decay * after
            found.append(after)
        after_all = jnp.concatenate(found[::-1], axis=0)
        aft_ref[g] = after_all
        a_hi, a_lo = split(after_all)
        g_hi, g_lo = split(g_ref[g])
        none = jnp.zeros((16, B), bf16)
        far_w = jnp.concatenate(
            [g_hi, none, none, g_lo] + [none] * 4 + [g_hi] + [none] * 7, axis=0
        )
        far = mm(jnp.concatenate([a_hi, a_lo], axis=1), far_w, NN)
        skip = skip_ref[rows, :]
        direct = jnp.concatenate([skip] * (nb + 1), axis=0) * lhs.astype(f32)
        gml_ref[g] = near + far + direct


def moments_kernel(
    nb, h_ref, hp_ref, inv_ref, gain_ref, ct_ref, w_ref, ee_ref, d_ref, aft_ref,
    x_ref, skip_ref, corr_ref, mom_ref, end_ref,
):
    row, lane = iotas((B, B))
    upper = lane >= row
    step_lane = lax.broadcasted_iota(jnp.int32, (16, B), 1)
    togo = (B - step_lane).astype(f32)
    second = (step_lane >= 16) & (step_lane < 32)
    zeros = jnp.zeros((16, B), f32)
    for g in range(GB):
        rows = pl.ds(16 * g, 16)
        gain = gain_ref[rows, :]
        units = []
        for b in range(nb + 1):
            h = hp_ref[rows, :] if b == 0 else h_ref[rows, pl.ds(B * (b - 1), B)]
            inv = jnp.broadcast_to(inv_ref[pl.ds(b, 1), :], (16, B))
            units.append((h.astype(f32) * inv * gain).astype(bf16))
        x_all = jnp.concatenate(units, axis=0)
        x_ref[g] = x_all
        lhs = jnp.concatenate([x_all[: 16 * nb], x_all[16:]], axis=1)
        taps = toeplitz(w_ref[pl.ds(g, 1), :])
        cur = jnp.where(upper, taps, 0.0).astype(bf16)
        prev = jnp.where(upper, 0.0, taps).astype(bf16)
        mixed = mm(lhs, jnp.concatenate([prev, cur], axis=0), NN).astype(bf16)
        ct = jnp.concatenate([ct_ref[rows, pl.ds(B * b, B)] for b in range(nb)], axis=0)
        direct = ct.astype(f32) * mixed.astype(f32)
        total = direct[:16]
        for b in range(1, nb):
            total = total + direct[16 * b : 16 * b + 16]
        skip_ref[rows, :] = total
        pairs = mm(mixed, ct, TN)
        corr_ref[pl.ds(g, 1), :] = lag_sums(jnp.where(upper, pairs, 0.0))
        ee = ee_ref[g]
        weights = jnp.concatenate([ee, ee, ee, ee * togo, zeros, zeros, zeros, zeros], axis=0)
        hi, lo = split(weights)
        lifted = mm(
            jnp.concatenate([mixed, mixed], axis=1), jnp.concatenate([hi, lo], axis=1), NT
        )
        after = aft_ref[g]
        decay = jnp.broadcast_to(d_ref[pl.ds(g, 1), :], (16, B))
        plain = zeros
        scaled = zeros
        end = zeros
        for b in range(nb):
            lift = lifted[16 * b : 16 * b + 16]
            prod = lift * after[16 * b : 16 * b + 16]
            plain = plain + prod
            scaled = scaled + prod * float(B * (b + 1))
            end = decay * (end + jnp.where(second, lift * float(B * (nb - b)), lift))
        mom_ref[g] = jnp.concatenate(
            [plain[:8] + plain[8:], scaled[:8] + scaled[8:]], axis=0
        )
        end_ref[g] = end


def inputs_kernel(
    nb, gml_ref, a_ref, g_ref, dq_ref, h_ref, inv_ref, gain_ref, w_ref, x_ref,
    ig_ref, row_ref, gain_out_ref, tap_ref,
):
    row, lane = iotas((B, B))
    upper = lane >= row
    lower = row >= lane

    @pl.when(pl.program_id(0) == 0)
    def _():
        row_ref[...] = jnp.zeros_like(row_ref)

    sums = [row_ref[pl.ds(8 * b, 8), :] for b in range(nb)]
    for g in range(GB):
        rows = pl.ds(16 * g, 16)
        q = g % 4
        if q == 0:
            decay = jnp.broadcast_to(dq_ref[g // 4], (16, B))
            after = a_ref[g // 4]
            found = [after]
            for b in range(nb):
                after = after * decay
                found.append(after)
            after_all = jnp.concatenate(found[::-1], axis=0)
            a_hi, a_lo = split(after_all)
            a_lhs = jnp.concatenate([a_hi, a_lo, a_hi], axis=1)
        g_hi, g_lo = split(g_ref[g])
        none = jnp.zeros((16, B), bf16)
        pad = [none] * (2 * q)
        end = [none] * (7 - 2 * q)
        far_w = jnp.concatenate(
            pad + [g_hi] + end + pad + [g_hi] + end + pad + [g_lo] + end, axis=0
        )
        grad = (gml_ref[g] + mm(a_lhs, far_w, NN)).astype(bf16)
        taps = toeplitz(w_ref[pl.ds(g, 1), :])
        cur = jnp.where(upper, taps, 0.0).astype(bf16)
        prev = jnp.where(upper, 0.0, taps).astype(bf16)
        lhs = jnp.concatenate([grad[: 16 * nb], grad[16:]], axis=1)
        ig = mm(lhs, jnp.concatenate([cur, prev], axis=1), NT)
        ig_ref[g] = ig
        gain = gain_ref[rows, :]
        part = jnp.zeros((16, B), f32)
        for b in range(nb):
            h = h_ref[rows, pl.ds(B * b, B)].astype(f32)
            prod = ig[16 * b : 16 * b + 16] * h
            inv = jnp.broadcast_to(inv_ref[pl.ds(b + 1, 1), :], (16, B))
            part = part + prod * inv
            prod = prod * gain
            sums[b] = sums[b] + (prod[:8] + prod[8:])
        gain_out_ref[rows, :] = part
        x_all = x_ref[g]
        x_pair = jnp.concatenate([x_all[16:], x_all[: 16 * nb]], axis=1)
        pairs = mm(grad[: 16 * nb], x_pair, TN)
        tap_ref[pl.ds(g, 1), :] = lag_sums(jnp.where(lower, pairs[:, :B], pairs[:, B:]))
    for b in range(nb):
        row_ref[pl.ds(8 * b, 8), :] = sums[b]


def final_kernel(nb, width, ig_ref, h_ref, inv_ref, gain_ref, raw_ref, out_ref):
    for g in range(GB):
        rows = pl.ds(16 * g, 16)
        gain = gain_ref[rows, :]
        for b in range(nb):
            cols = pl.ds(B * b, B)
            inv = inv_ref[pl.ds(b + 1, 1), :]
            pull = raw_ref[pl.ds(b, 1), :] * inv * inv * (1.0 / width)
            h = h_ref[rows, cols].astype(f32)
            ig = ig_ref[g, pl.ds(16 * b, 16), :]
            out_ref[rows, cols] = (inv * (ig * gain - h * pull)).astype(bf16)


def scan_kernel(count, span, s_ref, r_ref, out_ref):
    lane = lax.broadcasted_iota(jnp.int32, (8, B), 1)
    ones = (lane % 32) >= 16
    decay = jnp.exp(jnp.broadcast_to(r_ref[...], (8, B)) * (-float(span)))
    x = jnp.zeros((8, B), f32)
    found = [None] * count
    found[count - 1] = x
    for i in range(count - 2, -1, -1):
        x = s_ref[i + 1] + decay * x
        found[i] = x
    v = jnp.zeros((8, B), f32)
    out_ref[count - 1] = x * 0.0
    for i in range(count - 2, -1, -1):
        v = decay * (v + float(span) * pltpu.roll(found[i + 1], 16, 1))
        out_ref[i] = found[i] + jnp.where(ones, v, 0.0)


def call(kernel, name, grid, ins, outs, args, flops=0, moved=0):
    return pl.pallas_call(
        kernel,
        name=name,
        grid=grid,
        in_specs=ins,
        out_specs=outs[0],
        out_shape=outs[1],
        compiler_params=pltpu.CompilerParams(vmem_limit_bytes=40 * 1024 * 1024),
        cost_estimate=pl.CostEstimate(flops=flops, bytes_accessed=moved, transcendentals=0),
    )(*args)


def ch_sum(x, count):
    seen = [x] + [
        lax.ppermute(x, "ch", [(i, i ^ k) for i in range(count)]) for k in range(1, count)
    ]
    while len(seen) > 1:
        seen = [seen[i] + seen[i + 1] for i in range(0, len(seen), 2)]
    return seen[0]


def ctx_sum(x, count):
    parts = lax.all_to_all(x.reshape(count, -1), "ctx", 0, 0, tiled=True)
    mine = jnp.sum(parts, axis=0, keepdims=True)
    return lax.all_to_all(
        jnp.broadcast_to(mine, parts.shape), "ctx", 0, 0, tiled=True
    ).reshape(x.shape)


def local(hidden, cotangent, norm_gain, mr_filter, residue, decay_rate, skip_weight):
    channels, tokens = hidden.shape
    groups, taps = mr_filter.shape
    modes = residue.shape[1]
    n_ctx = lax.axis_size("ctx")
    n_ch = lax.axis_size("ch")
    width = channels * n_ch
    scale = (tokens * n_ctx) ** (-0.5)
    nb = tokens // B
    grid = (groups // GB,)

    h_prev = lax.ppermute(hidden[:, tokens - B :], "ctx", [(i, i + 1) for i in range(n_ctx - 1)])
    ct_next = lax.ppermute(cotangent[:, :B], "ctx", [(i, i - 1) for i in range(1, n_ctx)])

    own_sq = jnp.sum(jnp.square(hidden.astype(f32)), axis=0).reshape(nb, B)
    edge_sq = jnp.sum(jnp.square(h_prev.astype(f32)), axis=0).reshape(1, B)
    squares = ch_sum(jnp.concatenate([edge_sq, own_sq], axis=0), n_ch)
    inverse = lax.rsqrt(squares / width + eps_norm)

    steps = jnp.arange(B, dtype=f32)
    amplitude = residue * jnp.sqrt(2.0 * decay_rate)
    e0 = jnp.exp(-decay_rate[:, :, None] * steps)
    ee = jnp.exp(-decay_rate[:, :, None] * (B - steps))
    g_table = amplitude[:, :, None] * ee
    k_table = jnp.sum(amplitude[:, :, None] * e0, axis=1)
    block_decay = jnp.exp(-decay_rate * B)
    d_table = jnp.tile(block_decay, (1, 8))
    dq_table = jnp.concatenate([block_decay, block_decay], axis=1).reshape(groups // 4, 1, B)
    gain_wide = jnp.broadcast_to(norm_gain[:, None], (channels, B))
    skip_wide = jnp.broadcast_to(skip_weight[:, None], (channels, B))

    wide = pl.BlockSpec((16 * GB, tokens), lambda i: (i, 0))
    thin = pl.BlockSpec((16 * GB, B), lambda i: (i, 0))
    per_mode = pl.BlockSpec((GB, 16, B), lambda i: (i, 0, 0))
    vector = pl.BlockSpec((GB, B), lambda i: (i, 0))
    tall = pl.BlockSpec((GB, 16 * (nb + 1), B), lambda i: (i, 0, 0))
    body = pl.BlockSpec((GB, 16 * nb, B), lambda i: (i, 0, 0))
    quad = pl.BlockSpec((GB // 4, 16, B), lambda i: (i, 0, 0))
    quad_row = pl.BlockSpec((GB // 4, 1, B), lambda i: (i, 0, 0))
    inv_spec = pl.BlockSpec((nb + 1, B), lambda i: (0, 0))
    row_spec = pl.BlockSpec((8 * nb, B), lambda i: (0, 0))
    raw_spec = pl.BlockSpec((nb, B), lambda i: (0, 0))
    shape = jax.ShapeDtypeStruct
    tall_f32 = shape((groups, 16 * (nb + 1), B), f32)

    grad_local, after_local = call(
        functools.partial(grads_kernel, nb),
        "grads",
        grid,
        [wide, thin, per_mode, per_mode, vector, vector, thin],
        ([tall, tall], [tall_f32, tall_f32]),
        (cotangent, ct_next, e0, g_table, k_table, d_table, skip_wide),
        flops=groups * 2 * 144 * 256 * 384,
        moved=14 * 2**20,
    )

    head = after_local[:, :16, :]
    state_zero = head[:, :, :16]
    state_one = head[:, :, 16:32] + head[:, :, 32:48] - B * state_zero
    packed = jnp.concatenate([state_zero, state_one], axis=2)
    packed = packed.reshape(groups // 4, 4, 16, 32).transpose(0, 2, 1, 3).reshape(n_ctx, 8, B)
    arrived = lax.all_to_all(packed, "ctx", 0, 0, tiled=True)
    rate_rows = jnp.concatenate([decay_rate, decay_rate], axis=1).reshape(groups // 4, B)
    my_rates = lax.dynamic_slice_in_dim(rate_rows, lax.axis_index("ctx") // 2, 1, 0)
    whole = pl.BlockSpec((n_ctx, 8, B), lambda: (0, 0, 0))
    scanned = call(
        functools.partial(scan_kernel, n_ctx, tokens),
        "scan",
        (),
        [whole, pl.BlockSpec((1, B), lambda: (0, 0))],
        (whole, shape((n_ctx, 8, B), f32)),
        (arrived, my_rates),
        moved=2**18,
    )
    after = lax.all_to_all(scanned, "ctx", 0, 0, tiled=True).reshape(groups // 4, 16, B)

    units, skip_part, corr, mom, ends = call(
        functools.partial(moments_kernel, nb),
        "moments",
        grid,
        [wide, thin, inv_spec, thin, wide, vector, per_mode, vector, tall],
        (
            [tall, thin, vector, per_mode, per_mode],
            [
                shape((groups, 16 * (nb + 1), B), bf16),
                shape((channels, B), f32),
                shape((groups, B), f32),
                shape((groups, 16, B), f32),
                shape((groups, 16, B), f32),
            ],
        ),
        (
            hidden, h_prev, inverse, gain_wide, cotangent, mr_filter.astype(f32), ee, d_table,
            after_local,
        ),
        flops=groups * 2 * 128 * 256 * 384,
        moved=14 * 2**20,
    )

    ig, row_part, gain_part, tap_part = call(
        functools.partial(inputs_kernel, nb),
        "inputs",
        grid,
        [tall, quad, per_mode, quad_row, wide, inv_spec, thin, vector, tall],
        (
            [body, row_spec, thin, vector],
            [
                shape((groups, 16 * nb, B), f32),
                shape((8 * nb, B), f32),
                shape((channels, B), f32),
                shape((groups, B), f32),
            ],
        ),
        (
            grad_local, after, g_table, dq_table, hidden, inverse, gain_wide,
            mr_filter.astype(f32), units,
        ),
        flops=groups * 2 * 144 * 256 * 512,
        moved=14 * 2**20,
    )

    raw = ch_sum(jnp.sum(row_part.reshape(nb, 8, B), axis=1), n_ch)
    grad_hidden = call(
        functools.partial(final_kernel, nb, width),
        "final",
        grid,
        [body, wide, inv_spec, thin, raw_spec],
        (wide, shape((channels, tokens), bf16)),
        (ig, hidden, inverse, gain_wide, raw),
        moved=8 * 2**20,
    )
    grad_inv_rms = (raw * width ** (-0.5)).reshape(tokens)

    after_g = after.reshape(groups // 4, 16, 4, 32).transpose(0, 2, 1, 3).reshape(groups, 16, 32)
    a_zero, a_one = after_g[:, :, :16], after_g[:, :, 16:]
    end_zero = ends[:, :, :16]
    end_one = ends[:, :, 16:32] + ends[:, :, 48:64]
    plain = jnp.sum(mom[:, :8], axis=1)
    scaled = jnp.sum(mom[:, 8:], axis=1)
    near = corr[:, None, :] * e0
    first = jnp.sum(near, axis=2) + plain[:, :16] + jnp.sum(end_zero * a_zero, axis=1)
    second = (
        jnp.sum(near * steps, axis=2)
        + plain[:, 16:32] + plain[:, 32:48] + plain[:, 48:64] - scaled[:, :16]
        + jnp.sum(end_one * a_zero + end_zero * a_one, axis=1)
    )
    flipped = jnp.concatenate([tap_part[:, :1], tap_part[:, :0:-1]], axis=1)
    payload = jnp.concatenate(
        [
            flipped.reshape(-1),
            jnp.sum(gain_part, axis=1),
            jnp.sum(skip_part, axis=1),
            first.reshape(-1),
            second.reshape(-1),
        ]
    )
    total = ctx_sum(payload, n_ctx)
    cuts = [groups * taps, channels, channels, groups * modes, groups * modes]
    pieces = []
    start = 0
    for size in cuts:
        pieces.append(total[start : start + size])
        start += size
    first_total = pieces[3].reshape(groups, modes)
    second_total = pieces[4].reshape(groups, modes)
    root_rate = jnp.sqrt(2.0 * decay_rate)
    return (
        grad_hidden,
        pieces[1] * scale,
        pieces[0].reshape(groups, taps) * scale,
        root_rate * first_total * scale,
        residue * root_rate * (0.5 * first_total - decay_rate * second_total) * scale,
        pieces[2] * scale,
        grad_inv_rms,
    )


def solution(mesh):
    return jax.shard_map(
        local,
        mesh=mesh,
        in_specs=(
            P("ch", "ctx"),
            P("ch", "ctx"),
            P("ch"),
            P("ch", None),
            P("ch", None),
            P("ch", None),
            P("ch"),
        ),
        out_specs=(
            P("ch", "ctx"),
            P("ch"),
            P("ch", None),
            P("ch", None),
            P("ch", None),
            P("ch"),
            P("ctx"),
        ),
        check_vma=False,
    )
```

```python
import functools

import jax
import jax.numpy as jnp
from jax import lax
from jax.experimental import pallas as pl
from jax.experimental.pallas import tpu as pltpu
from jax.sharding import PartitionSpec as P

eps_norm = 1e-06
B = 128
GB = 8
VMEM = 16 * 1024 * 1024
f32 = jnp.float32
bf16 = jnp.bfloat16

NN = (((1,), (0,)), ((), ()))
NT = (((1,), (1,)), ((), ()))
TN = (((0,), (0,)), ((), ()))


def mm(a, b, dims):
    return lax.dot_general(a, b, dims, preferred_element_type=f32)


def split(x):
    hi = x.astype(bf16)
    lo = (x - hi.astype(f32)).astype(bf16)
    return hi, lo


def iotas(shape):
    return (
        lax.broadcasted_iota(jnp.int32, shape, 0),
        lax.broadcasted_iota(jnp.int32, shape, 1),
    )


def spread(row):
    return jnp.transpose(jnp.broadcast_to(row, (B, B)))


def fine(x):
    hi, mid = split(x)
    low = (x - hi.astype(f32) - mid.astype(f32)).astype(bf16)
    return jnp.concatenate([hi, mid, low], axis=1)


def lane_sums(x):
    return mm(jnp.ones((8, 3 * B), bf16), fine(x), NT)[:1]


def toeplitz(row):
    full = jnp.broadcast_to(row, (B, B))
    return pltpu.roll(full, 0, 1, stride=1, stride_axis=0)


def lag_sums(square):
    total = square[:8]
    for a in range(8, B, 8):
        total = total + pltpu.roll(square[a : a + 8], B - a, 1)
    row = lax.broadcasted_iota(jnp.int32, (8, B), 0)
    for bit in (1, 2, 4):
        total = jnp.where((row & bit) != 0, pltpu.roll(total, B - bit, 1), total)
    return jnp.sum(total, axis=0, keepdims=True)


def prep_kernel(h_ref, ct_ref, tail_ref, head_ref, sq_ref, acc_ref):
    tokens = h_ref.shape[1]

    @pl.when(pl.program_id(0) == 0)
    def _():
        acc_ref[...] = jnp.zeros_like(acc_ref)

    h = h_ref[...].astype(f32)
    acc_ref[...] += jnp.sum(jnp.square(h).reshape(h.shape[0] // 8, 8, tokens), axis=0)
    tail_ref[...] = h_ref[:, tokens - B :]
    head_ref[...] = ct_ref[...]

    @pl.when(pl.program_id(0) == pl.num_programs(0) - 1)
    def _():
        row = jnp.sum(acc_ref[...], axis=0, keepdims=True)
        for b in range(tokens // B):
            sq_ref[pl.ds(b, 1), :] = row[:, B * b : B * b + B]


def edge_kernel(nb, h_ref, sq_ref, out_ref):
    h = h_ref[...].astype(f32)
    part = jnp.sum(jnp.square(h).reshape(h.shape[0] // 8, 8, B), axis=0)
    edge = jnp.sum(part, axis=0, keepdims=True)
    rows = jnp.concatenate([edge, sq_ref[...], jnp.zeros((7, B), f32)], axis=0)
    for i in range(out_ref.shape[0]):
        out_ref[i] = rows


def inverse_rows(sq_ref, width):
    total = sq_ref[0]
    for i in range(1, sq_ref.shape[0]):
        total = total + sq_ref[i]
    return lax.rsqrt(total / width + eps_norm)


def grads_kernel(
    nb, ct_ref, ctn_ref, rate_ref, res_ref, four_ref, skip_ref, gml_ref, aft_ref, pack_ref
):
    step = pl.program_id(0)
    row, lane = iotas((B, B))
    upper = lane <= row
    back = ((B - lane) % B).astype(f32)
    below = row.astype(f32)
    slot = lane % 64
    first_half = lane < 64
    step_lane = lax.broadcasted_iota(jnp.int32, (16, B), 1)
    step_slot = step_lane % 64
    third = (step_slot >= 32) & (step_slot < 48)
    zeros = jnp.zeros((16, B), f32)
    none = jnp.zeros((16, B), bf16)
    rates = spread(rate_ref[pl.ds(step, 1), :])
    amps = spread(res_ref[pl.ds(step, 1), :]) * jnp.sqrt(2.0 * rates)
    reach = amps * jnp.exp(-rates * (float(B) - lane.astype(f32)))
    lags = amps * jnp.exp(-rates * back)
    skips = spread(skip_ref[pl.ds(step, 1), :])

    def near_part(g, fall):
        rows = pl.ds(16 * g, 16)
        sub = slice(16 * g, 16 * g + 16)
        blocks = [ct_ref[rows, pl.ds(B * b, B)] for b in range(nb)] + [ctn_ref[rows, :]]
        lhs = jnp.concatenate(blocks, axis=0)
        kernel_row = jnp.sum(lags[sub], axis=0, keepdims=True)
        toe = jnp.where(upper, toeplitz(kernel_row), 0.0)
        mine = jnp.where(first_half if g % 2 == 0 else ~first_half, fall, 0.0)
        hi, lo = split(jnp.concatenate([toe, mine], axis=1))
        out = mm(jnp.concatenate([lhs, lhs], axis=1), jnp.concatenate([hi, lo], axis=0), NN)
        direct = jnp.concatenate([skips[sub]] * (nb + 1), axis=0) * lhs.astype(f32)
        gml_ref[g] = out[:, :B] + direct
        return out[:, B:]

    def first_stage(p):
        pair_rates = four_ref[pl.ds(4 * step + p, 1), :]
        fall = jnp.exp(-pair_rates * below)
        fall = jnp.where((slot >= 16) & (slot < 32), fall * below, fall)
        return near_part(2 * p, fall) + near_part(2 * p + 1, fall), pair_rates

    def second_stage(p, states, pair_rates):
        decay = jnp.broadcast_to(jnp.exp(-pair_rates * float(B)), (16, B))
        after = zeros
        found = [after]
        for b in range(nb, 0, -1):
            state = states[16 * b : 16 * b + 16]
            state = jnp.where(third, state * float(B * b), state)
            after = state + decay * after
            found.append(after)
        after_all = jnp.concatenate(found[::-1], axis=0)
        aft_ref[p] = after_all
        one = after + pltpu.roll(after, B - 16, 1) - float(B) * pltpu.roll(after, 16, 1)
        tile = jnp.where(step_slot < 16, after, jnp.where(step_slot < 32, one, 0.0))
        tile = tile + pltpu.roll(tile, B - 32, 1)
        tile = jnp.where(step_lane < 64, tile, 0.0)
        a_hi, a_lo = split(after_all)
        halves = []
        for h in range(2):
            g = 2 * p + h
            g_hi, g_lo = split(reach[16 * g : 16 * g + 16])
            upper_rows = [g_hi, none, none, g_lo]
            lower_rows = [g_hi, none, none, none]
            gap = [none] * 4
            if h == 0:
                parts = upper_rows + gap + lower_rows + gap
            else:
                parts = gap + upper_rows + gap + lower_rows
            halves.append(jnp.concatenate(parts, axis=0))
        far = mm(
            jnp.concatenate([a_hi, a_lo], axis=1), jnp.concatenate(halves, axis=1), NN
        )
        gml_ref[2 * p] += far[:, :B]
        gml_ref[2 * p + 1] += far[:, B:]
        return tile

    held = first_stage(0)
    tiles = []
    for p in range(GB // 2):
        ahead = first_stage(p + 1) if p + 1 < GB // 2 else None
        tiles.append(second_stage(p, *held))
        held = ahead
    for k in range(GB // 4):
        pack_ref[k] = tiles[2 * k] + pltpu.roll(tiles[2 * k + 1], 64, 1)


def squeeze(tile):
    lane = lax.broadcasted_iota(jnp.int32, tile.shape, 1)
    tile = jnp.where(lane % 64 < 32, tile, 0.0)
    return jnp.where(lane < 64, tile + pltpu.roll(tile, B - 32, 1), 0.0)


def moments_kernel(
    nb, width, offset, h_ref, hp_ref, sq_ref, gain_ref, ct_ref, w_ref, rate_ref, four_ref,
    aft_ref, *refs,
):
    x_ref, part_ref, end_ref, w_scratch = refs[-4:]
    step = pl.program_id(0) + offset

    @pl.when(step == offset)
    def _():
        w_scratch[...] = w_ref[...].astype(f32)

    row, lane = iotas((B, B))
    upper = lane >= row
    ahead = lane.astype(f32)
    togo = float(B) - row.astype(f32)
    slot = lane % 64
    first_half = lane < 64
    step_slot = lax.broadcasted_iota(jnp.int32, (16, B), 1) % 64
    low = step_slot < 16
    half = step_slot < 32
    second = half & (step_slot >= 16)
    zeros = jnp.zeros((16, B), f32)
    inverse = inverse_rows(sq_ref, width)
    gains = spread(gain_ref[pl.ds(step, 1), :])

    def mix(g):
        rows = pl.ds(16 * g, 16)
        sub = slice(16 * g, 16 * g + 16)
        units = []
        for b in range(nb + 1):
            h = hp_ref[rows, :] if b == 0 else h_ref[rows, pl.ds(B * (b - 1), B)]
            units.append((h.astype(f32) * inverse[b : b + 1] * gains[sub]).astype(bf16))
        x_all = jnp.concatenate(units, axis=0)
        x_ref[g] = x_all
        lhs = jnp.concatenate([x_all[: 16 * nb], x_all[16:]], axis=1)
        taps = toeplitz(w_scratch[pl.ds(GB * step + g, 1), :])
        cur = jnp.where(upper, taps, 0.0).astype(bf16)
        prev = jnp.where(upper, 0.0, taps).astype(bf16)
        return mm(lhs, jnp.concatenate([prev, cur], axis=0), NN).astype(bf16)

    def first_stage(p):
        pair_rates = four_ref[pl.ds(4 * step + p, 1), :]
        rise = jnp.exp(-pair_rates * togo)
        rise = jnp.where(slot >= 48, rise * togo, rise)
        hi, lo = split(
            jnp.concatenate(
                [jnp.where(first_half, rise, 0.0), jnp.where(first_half, 0.0, rise)], axis=0
            )
        )
        mixes = [mix(2 * p), mix(2 * p + 1)]
        lifted = mm(
            jnp.concatenate(mixes, axis=1), jnp.concatenate([hi, lo], axis=1), NN
        )
        return mixes, lifted[:, :B] + lifted[:, B:], pair_rates

    skip_parts = []
    corrs = []

    def second_stage(p, mixes, lifted, pair_rates):
        for h in range(2):
            rows = pl.ds(16 * (2 * p + h), 16)
            mixed = mixes[h]
            ct = jnp.concatenate([ct_ref[rows, pl.ds(B * b, B)] for b in range(nb)], axis=0)
            pairs = mm(mixed, ct, TN)
            direct = ct.astype(f32) * mixed.astype(f32)
            total = direct[:16]
            for b in range(1, nb):
                total = total + direct[16 * b : 16 * b + 16]
            skip_parts.append(total)
            corrs.append(lag_sums(jnp.where(upper, pairs, 0.0)))
        after = aft_ref[p]
        decay = jnp.broadcast_to(jnp.exp(-pair_rates * float(B)), (16, B))
        plain = zeros
        scaled = zeros
        end = zeros
        for b in range(nb):
            lift = lifted[16 * b : 16 * b + 16]
            prod = lift * after[16 * b : 16 * b + 16]
            plain = plain + prod
            scaled = scaled + prod * float(B * (b + 1))
            end = decay * (end + jnp.where(second, lift * float(B * (nb - b)), lift))
        plain = plain[:8] + plain[8:]
        scaled = scaled[:8] + scaled[8:]
        after_one = (
            plain + pltpu.roll(plain, B - 16, 1) + pltpu.roll(plain, B - 32, 1)
            - pltpu.roll(scaled, 16, 1)
        )
        found = squeeze(jnp.where(low[:8], plain, after_one))
        ends_zero = squeeze(jnp.where(low, end, pltpu.roll(end, B - 16, 1)))
        ends_one = squeeze(
            jnp.where(low, pltpu.roll(end, B - 16, 1) + pltpu.roll(end, B - 48, 1), 0.0)
        )
        return found, ends_zero, ends_one

    held = first_stage(0)
    tiles = []
    for p in range(GB // 2):
        nxt = first_stage(p + 1) if p + 1 < GB // 2 else None
        tiles.append(second_stage(p, *held))
        held = nxt
    quads = []
    for k in range(GB // 4):
        left, right = tiles[2 * k], tiles[2 * k + 1]
        joined = [a + pltpu.roll(b, 64, 1) for a, b in zip(left, right)]
        quads.append(jnp.sum(joined[0], axis=0, keepdims=True))
        end_ref[k] = jnp.concatenate(joined[1:], axis=0)
    skip_row = lane_sums(jnp.concatenate(skip_parts, axis=0))
    corr = jnp.concatenate(corrs, axis=0)
    fall = jnp.exp(-spread(rate_ref[pl.ds(step, 1), :]) * ahead)
    table = []
    for g in range(GB):
        table += [fall[16 * g : 16 * g + 16], fall[16 * g : 16 * g + 16] * ahead[:16]]
    t_hi, t_lo = split(jnp.concatenate(table, axis=0))
    c_hi, c_lo = split(corr)
    near = mm(
        jnp.concatenate([c_hi, c_lo, c_hi], axis=1),
        jnp.concatenate([t_hi, t_hi, t_lo], axis=1),
        NT,
    )
    n_row, n_lane = iotas((GB, 32 * GB))
    near = jnp.sum(jnp.where(n_lane // 32 == n_row, near, 0.0), axis=0, keepdims=True)
    blank = jnp.zeros((1, B), f32)
    part_ref[...] = jnp.concatenate(
        [blank] * 6 + [skip_row] + [blank] * 3 + [quads[0] + near[:, :B]]
        + [blank] * 3 + [quads[1] + near[:, B:]] + [blank],
        axis=0,
    )


def mirror_matrix():
    row, lane = iotas((B, B))
    return jnp.where((row + lane) % B == 0, 1.0, 0.0).astype(bf16)


def inputs_kernel(
    nb, width, gml_ref, a_ref, rate_ref, res_ref, pair_ref, h_ref, sq_ref, gain_ref, w_ref,
    part_ref, end_ref, ig_ref, row_ref, pay_ref, grad_ref, acc_ref, w_scratch,
):
    step = pl.program_id(0)

    @pl.when(step == 0)
    def _():
        w_scratch[...] = mm(w_ref[...], mirror_matrix(), NN)
        acc_ref[...] = jnp.zeros_like(acc_ref)

    row, lane = iotas((B, B))
    upper = lane <= row
    none = jnp.zeros((16, B), bf16)
    ones = (lax.broadcasted_iota(jnp.int32, (16, B), 1) % 32) >= 16
    inverse = inverse_rows(sq_ref, width)
    gains = spread(gain_ref[pl.ds(step, 1), :])
    rates = spread(rate_ref[pl.ds(step, 1), :])
    amps = spread(res_ref[pl.ds(step, 1), :]) * jnp.sqrt(2.0 * rates)
    reach = amps * jnp.exp(-rates * (float(B) - lane.astype(f32)))
    sums = [acc_ref[pl.ds(8 * b, 8), :] for b in range(nb)]
    gain_parts = []
    quads = []
    lhs_of = {}

    def cross(k):
        decay = jnp.exp(jnp.broadcast_to(pair_ref[k], (16, B)) * (-float(B)))
        after = a_ref[k]
        ends = end_ref[k]
        first = jnp.sum(ends[:16] * after, axis=0, keepdims=True)
        other = jnp.sum(ends[16:] * after, axis=0, keepdims=True)
        quads.append(first + pltpu.roll(jnp.broadcast_to(other, (8, B)), 16, 1)[:1])
        after = jnp.where(ones, pltpu.roll(after, 16, 1), after)
        found = [after]
        for b in range(nb):
            after = after * decay
            found.append(after)
        a_hi, a_lo = split(jnp.concatenate(found[::-1], axis=0))
        return jnp.concatenate([a_hi, a_lo], axis=1)

    def first_stage(p):
        k = p // 2
        if k not in lhs_of:
            lhs_of[k] = cross(k)
        halves = []
        for h in range(2):
            g = 2 * p + h
            q = g % 4
            g_hi, g_lo = split(reach[16 * g : 16 * g + 16])
            pad = [none] * (2 * q)
            end = [none] * (6 - 2 * q)
            halves.append(
                jnp.concatenate(pad + [g_hi, g_lo] + end + pad + [g_hi, none] + end, axis=0)
            )
        far = mm(lhs_of[k], jnp.concatenate(halves, axis=1), NN)
        grads = []
        for h in range(2):
            g = 2 * p + h
            grad = (gml_ref[g] + far[:, B * h : B * h + B]).astype(bf16)
            grad_ref[g] = grad[: 16 * nb]
            grads.append(grad)
        return grads

    def second_stage(p, grads):
        for h in range(2):
            g = 2 * p + h
            rows = pl.ds(16 * g, 16)
            sub = slice(16 * g, 16 * g + 16)
            grad = grads[h]
            taps = toeplitz(w_scratch[pl.ds(GB * step + g, 1), :])
            cur = jnp.where(upper, taps, 0.0).astype(bf16)
            prev = jnp.where(upper, 0.0, taps).astype(bf16)
            lhs = jnp.concatenate([grad[: 16 * nb], grad[16:]], axis=1)
            ig = mm(lhs, jnp.concatenate([cur, prev], axis=0), NN)
            ig_ref[g] = ig
            part = jnp.zeros((16, B), f32)
            for b in range(nb):
                prod = ig[16 * b : 16 * b + 16] * h_ref[rows, pl.ds(B * b, B)].astype(f32)
                part = part + prod * inverse[b + 1 : b + 2]
                prod = prod * gains[sub]
                sums[b] = sums[b] + (prod[:8] + prod[8:])
            gain_parts.append(part)

    held = first_stage(0)
    for p in range(GB // 2):
        nxt = first_stage(p + 1) if p + 1 < GB // 2 else None
        second_stage(p, held)
        held = nxt
    for b in range(nb):
        acc_ref[pl.ds(8 * b, 8), :] = sums[b]
    gain_row = lane_sums(jnp.concatenate(gain_parts, axis=0))
    blank = jnp.zeros((1, B), f32)
    pay_ref[...] = part_ref[...] + jnp.concatenate(
        [blank, blank, gain_row] + [blank] * 7 + [quads[0]] + [blank] * 3 + [quads[1], blank],
        axis=0,
    )

    @pl.when(step == pl.num_programs(0) - 1)
    def _():
        raw = jnp.concatenate(
            [jnp.sum(sums[b], axis=0, keepdims=True) for b in range(nb)], axis=0
        )
        for i in range(row_ref.shape[0]):
            row_ref[i] = raw


def taps_kernel(nb, grad_ref, x_ref, pay_ref, out_ref):
    row, lane = iotas((B, B))
    lower = row >= lane

    def product(g):
        x_all = x_ref[g]
        x_pair = jnp.concatenate([x_all[16:], x_all[: 16 * nb]], axis=1)
        return mm(grad_ref[g], x_pair, TN)

    rows = []
    held = product(0)
    for g in range(GB):
        nxt = product(g + 1) if g + 1 < GB else None
        rows.append(lag_sums(jnp.where(lower, held[:, :B], held[:, B:])))
        held = nxt
    mirror = jnp.concatenate([mirror_matrix()] * 3, axis=0)
    taps = mm(fine(jnp.concatenate(rows, axis=0)), mirror, NN)
    blank = jnp.zeros((2, B), f32)
    out_ref[...] = pay_ref[...] + jnp.concatenate(
        [taps[0:2], blank, taps[2:4], blank, taps[4:6], blank, taps[6:8], blank], axis=0
    )


def final_kernel(nb, width, ig_ref, h_ref, sq_ref, gain_ref, raw_ref, out_ref, rms_ref):
    step = pl.program_id(0)
    inverse = inverse_rows(sq_ref, width)
    gains = spread(gain_ref[pl.ds(step, 1), :])
    raw = raw_ref[0]
    for i in range(1, raw_ref.shape[0]):
        raw = raw + raw_ref[i]
    rms_ref[...] = raw * width ** (-0.5)
    inv = [inverse[b + 1 : b + 2] for b in range(nb)]
    pull = [raw[b : b + 1] * inv[b] * inv[b] * (1.0 / width) for b in range(nb)]
    for g in range(GB):
        rows = pl.ds(16 * g, 16)
        gain = gains[16 * g : 16 * g + 16]
        for b in range(nb):
            cols = pl.ds(B * b, B)
            h = h_ref[rows, cols].astype(f32)
            ig = ig_ref[g, pl.ds(16 * b, 16), :]
            out_ref[rows, cols] = (inv[b] * (ig * gain - h * pull[b])).astype(bf16)


def scan_kernel(count, span, s_ref, r_ref, out_ref):
    lane = lax.broadcasted_iota(jnp.int32, (8, B), 1)
    ones = (lane % 32) >= 16
    rates = r_ref[pl.ds(lax.axis_index("ctx") // 2, 1), :]
    decay = jnp.exp(jnp.broadcast_to(rates, (8, B)) * (-float(span)))
    x = jnp.zeros((8, B), f32)
    found = [None] * count
    found[count - 1] = x
    for i in range(count - 2, -1, -1):
        x = s_ref[i + 1] + decay * x
        found[i] = x
    v = jnp.zeros((8, B), f32)
    out_ref[count - 1] = v
    for i in range(count - 2, -1, -1):
        v = decay * (v + float(span) * pltpu.roll(found[i + 1], 16, 1))
        out_ref[i] = found[i] + jnp.where(ones, v, 0.0)


def sum_kernel(in_ref, out_ref):
    total = in_ref[0]
    for i in range(1, in_ref.shape[0]):
        total = total + in_ref[i]
    for i in range(out_ref.shape[0]):
        out_ref[i] = total


def outs_kernel(scale, in_ref, tap_ref, gain_ref, skip_ref, mom_ref):
    owners = tap_ref.shape[0] // 2
    steps = gain_ref.shape[0]
    for r in range(2):
        tap_ref[pl.ds(r, owners, stride=2), :] = in_ref[pl.ds(r, owners, stride=4), :] * scale
    gain_ref[...] = in_ref[pl.ds(2, steps, stride=16), :] * scale
    skip_ref[...] = in_ref[pl.ds(6, steps, stride=16), :] * scale
    for r in range(2):
        mom_ref[pl.ds(r, steps, stride=2), :] = (
            in_ref[pl.ds(10 + 4 * r, steps, stride=16), :] * scale
        )


def call(kernel, name, grid, ins, outs, args, flops=0, moved=0, scratch=(), aliases={}):
    return pl.pallas_call(
        kernel,
        name=name,
        grid=grid,
        in_specs=ins,
        out_specs=outs[0],
        out_shape=outs[1],
        scratch_shapes=scratch,
        input_output_aliases=aliases,
        compiler_params=pltpu.CompilerParams(vmem_limit_bytes=VMEM),
        cost_estimate=pl.CostEstimate(flops=flops, bytes_accessed=moved, transcendentals=0),
    )(*args)


def exchange(x, axis):
    return lax.all_to_all(x, axis, 0, 0, tiled=True)


def local(hidden, cotangent, norm_gain, mr_filter, residue, decay_rate, skip_weight):
    channels, tokens = hidden.shape
    groups, taps = mr_filter.shape
    modes = residue.shape[1]
    n_ctx = lax.axis_size("ctx")
    n_ch = lax.axis_size("ch")
    width = channels * n_ch
    scale = (tokens * n_ctx) ** (-0.5)
    nb = tokens // B
    steps = groups // GB
    grid = (steps,)
    shape = jax.ShapeDtypeStruct
    hidden, cotangent, mr_filter = (
        pltpu.with_memory_space_constraint(x, pltpu.HBM) for x in (hidden, cotangent, mr_filter)
    )

    wide = pl.BlockSpec((16 * GB, tokens), lambda i: (i, 0))
    thin = pl.BlockSpec((16 * GB, B), lambda i: (i, 0))
    tall = pl.BlockSpec((GB, 16 * (nb + 1), B), lambda i: (i, 0, 0))
    pair_tall = pl.BlockSpec((GB // 2, 16 * (nb + 1), B), lambda i: (i, 0, 0))
    body = pl.BlockSpec((GB, 16 * nb, B), lambda i: (i, 0, 0))
    quad = pl.BlockSpec((GB // 4, 16, B), lambda i: (i, 0, 0))
    quad_two = pl.BlockSpec((GB // 4, 32, B), lambda i: (i, 0, 0))
    quad_row = pl.BlockSpec((GB // 4, 1, B), lambda i: (i, 0, 0))
    pay = pl.BlockSpec((16, B), lambda i: (i, 0))

    def full(*dims):
        return pl.BlockSpec(dims, lambda *i: (0,) * len(dims))

    tail, head, own_sq = call(
        prep_kernel,
        "prep",
        grid,
        [wide, thin],
        (
            [thin, thin, full(nb, B)],
            [shape((channels, B), bf16), shape((channels, B), bf16), shape((nb, B), f32)],
        ),
        (hidden, cotangent),
        moved=3 * 2**20,
        scratch=[pltpu.VMEM((8, tokens), f32)],
    )
    ct_next = lax.ppermute(head, "ctx", [(i, i - 1) for i in range(1, n_ctx)])
    h_prev = lax.ppermute(tail, "ctx", [(i, i + 1) for i in range(n_ctx - 1)])
    edge = call(
        functools.partial(edge_kernel, nb),
        "edge",
        (),
        [full(channels, B), full(nb, B)],
        (full(n_ch, 16, B), shape((n_ch, 16, B), f32)),
        (h_prev, own_sq),
        moved=2**18,
    )
    edge, ct_next = lax.optimization_barrier((edge, ct_next))
    squares = exchange(edge, "ch")

    rate_flat = decay_rate.reshape(steps, B)
    res_flat = residue.reshape(steps, B)
    rate_four = jnp.tile(decay_rate, (1, 4)).reshape(groups // 2, B)
    rate_pair = jnp.concatenate([decay_rate, decay_rate], axis=1).reshape(groups // 4, B)
    gain_flat = norm_gain.reshape(steps, B)
    skip_flat = skip_weight.reshape(steps, B)
    flat = full(steps, B)

    grad_local, after_local, packed = call(
        functools.partial(grads_kernel, nb),
        "grads",
        grid,
        [wide, thin, flat, flat, full(groups // 2, B), flat],
        (
            [tall, pair_tall, quad],
            [
                shape((groups, 16 * (nb + 1), B), f32),
                shape((groups // 2, 16 * (nb + 1), B), f32),
                shape((groups // 4, 16, B), f32),
            ],
        ),
        (cotangent, ct_next, rate_flat, res_flat, rate_four, skip_flat),
        flops=groups * 2 * 144 * 256 * 384,
        moved=14 * 2**20,
    )

    def moments(offset, before, x_next):
        def at(spec):
            return pl.BlockSpec(
                spec.block_shape, lambda i: (i + offset,) + spec.index_map(i)[1:]
            )

        held = [pl.BlockSpec(memory_space=pl.ANY)] * len(before)
        return call(
            functools.partial(moments_kernel, nb, width, offset),
            "moments",
            (steps // 2,),
            [
                at(wide), at(thin), full(n_ch, 16, B), flat, at(wide), full(groups, B), flat,
                full(groups // 2, B), at(pair_tall),
            ]
            + held,
            (
                [at(tall), at(pay), at(quad_two)],
                [
                    shape((groups, 16 * (nb + 1), B), bf16),
                    shape((16 * steps, B), f32),
                    shape((groups // 4, 32, B), f32),
                ],
            ),
            (
                hidden, x_next, squares, gain_flat, cotangent, mr_filter, rate_flat, rate_four,
                after_local, *before,
            ),
            flops=groups * 128 * 256 * 384,
            moved=7 * 2**20,
            scratch=[pltpu.VMEM((groups, B), f32)],
            aliases={9 + i: i for i in range(len(before))},
        )

    arrived = exchange(packed.reshape(n_ctx, 8, B), "ctx")
    early = moments(0, (), h_prev)
    arrived, early = lax.optimization_barrier((arrived, tuple(early)))
    scanned = call(
        functools.partial(scan_kernel, n_ctx, tokens),
        "scan",
        (),
        [full(n_ctx, 8, B), full(groups // 4, B)],
        (full(n_ctx, 8, B), shape((n_ctx, 8, B), f32)),
        (arrived, rate_pair),
        moved=2**18,
    )
    scanned, edge_rows = lax.optimization_barrier((scanned, h_prev))
    after = exchange(scanned, "ctx").reshape(groups // 4, 16, B)
    units, part, ends = moments(steps // 2, early, edge_rows)

    ig, row_part, mostly, grad_mixed = call(
        functools.partial(inputs_kernel, nb, width),
        "inputs",
        grid,
        [
            tall, quad, flat, flat, quad_row, wide, full(n_ch, 16, B), flat, full(groups, B),
            pay, quad_two,
        ],
        (
            [body, full(n_ch, nb, B), pay, body],
            [
                shape((groups, 16 * nb, B), f32),
                shape((n_ch, nb, B), f32),
                shape((16 * steps, B), f32),
                shape((groups, 16 * nb, B), bf16),
            ],
        ),
        (
            grad_local, after, rate_flat, res_flat, rate_pair.reshape(groups // 4, 1, B), hidden,
            squares, gain_flat, mr_filter, part, ends,
        ),
        flops=groups * 2 * 144 * 256 * 512,
        moved=14 * 2**20,
        scratch=[pltpu.VMEM((8 * nb, B), f32), pltpu.VMEM((groups, B), f32)],
    )

    raw = exchange(row_part, "ch")
    payload = call(
        functools.partial(taps_kernel, nb),
        "taps",
        grid,
        [body, tall, pay],
        (pay, shape((16 * steps, B), f32)),
        (grad_mixed, units, mostly),
        flops=groups * 2 * 128 * 128 * 256,
        moved=5 * 2**20,
    )
    raw, payload = lax.optimization_barrier((raw, payload))
    landed = exchange(payload.reshape(n_ctx, 4, B), "ctx")
    grad_hidden, grad_inv_rms = call(
        functools.partial(final_kernel, nb, width),
        "final",
        grid,
        [body, wide, full(n_ch, 16, B), flat, full(n_ch, nb, B)],
        (
            [wide, full(nb, B)],
            [shape((channels, tokens), bf16), shape((nb, B), f32)],
        ),
        (ig, hidden, squares, gain_flat, raw),
        moved=8 * 2**20,
    )
    landed, grad_inv_rms = lax.optimization_barrier((landed, grad_inv_rms))
    chunk = full(n_ctx, 4, B)
    summed = call(
        sum_kernel, "sum", (), [chunk], (chunk, shape((n_ctx, 4, B), f32)), (landed,),
        moved=2**17,
    )
    total = exchange(summed, "ctx").reshape(4 * n_ctx, B)
    grad_mr, grad_gain, grad_skip, both = call(
        functools.partial(outs_kernel, scale),
        "outs",
        (),
        [full(4 * n_ctx, B)],
        (
            [full(groups, taps), full(steps, B), full(steps, B), full(groups // 4, B)],
            [
                shape((groups, taps), f32),
                shape((steps, B), f32),
                shape((steps, B), f32),
                shape((groups // 4, B), f32),
            ],
        ),
        (total,),
        moved=2**17,
    )
    both = both.reshape(groups, 2 * modes)
    first, second = both[:, :modes], both[:, modes:]
    root_rate = jnp.sqrt(2.0 * decay_rate)
    return (
        grad_hidden,
        grad_gain.reshape(channels),
        grad_mr,
        root_rate * first,
        residue * root_rate * (0.5 * first - decay_rate * second),
        grad_skip.reshape(channels),
        grad_inv_rms.reshape(tokens),
    )


def solution(mesh):
    return jax.shard_map(
        local,
        mesh=mesh,
        in_specs=(
            P("ch", "ctx"),
            P("ch", "ctx"),
            P("ch"),
            P("ch", None),
            P("ch", None),
            P("ch", None),
            P("ch"),
        ),
        out_specs=(
            P("ch", "ctx"),
            P("ch"),
            P("ch", None),
            P("ch", None),
            P("ch", None),
            P("ch"),
            P("ctx"),
        ),
        check_vma=False,
    )
```

```python
import functools

import jax
import jax.numpy as jnp
from jax import lax
from jax.experimental import pallas as pl
from jax.experimental.pallas import tpu as pltpu
from jax.sharding import PartitionSpec as P

eps_norm = 1e-06
B = 128
GB = 8
VMEM = 16 * 1024 * 1024
f32 = jnp.float32
bf16 = jnp.bfloat16

NN = (((1,), (0,)), ((), ()))
NT = (((1,), (1,)), ((), ()))
TN = (((0,), (0,)), ((), ()))


def mm(a, b, dims):
    return lax.dot_general(a, b, dims, preferred_element_type=f32)


def split(x):
    hi = x.astype(bf16)
    lo = (x - hi.astype(f32)).astype(bf16)
    return hi, lo


def iotas(shape):
    return (
        lax.broadcasted_iota(jnp.int32, shape, 0),
        lax.broadcasted_iota(jnp.int32, shape, 1),
    )


def spread(row):
    return jnp.transpose(jnp.broadcast_to(row, (B, B)))


def fine(x):
    hi, mid = split(x)
    low = (x - hi.astype(f32) - mid.astype(f32)).astype(bf16)
    return jnp.concatenate([hi, mid, low], axis=1)


def lane_sums(x):
    return mm(jnp.ones((8, 3 * B), bf16), fine(x), NT)[:1]


def toeplitz(row):
    full = jnp.broadcast_to(row, (B, B))
    return pltpu.roll(full, 0, 1, stride=1, stride_axis=0)


def lag_sums(square):
    total = square[:8]
    for a in range(8, B, 8):
        total = total + pltpu.roll(square[a : a + 8], B - a, 1)
    row = lax.broadcasted_iota(jnp.int32, (8, B), 0)
    for bit in (1, 2, 4):
        total = jnp.where((row & bit) != 0, pltpu.roll(total, B - bit, 1), total)
    return jnp.sum(total, axis=0, keepdims=True)


def prep_kernel(h_ref, ct_ref, tail_ref, head_ref, sq_ref, acc_ref):
    tokens = h_ref.shape[1]

    @pl.when(pl.program_id(0) == 0)
    def _():
        acc_ref[...] = jnp.zeros_like(acc_ref)

    h = h_ref[...].astype(f32)
    acc_ref[...] += jnp.sum(jnp.square(h).reshape(h.shape[0] // 8, 8, tokens), axis=0)
    tail_ref[...] = h_ref[:, tokens - B :]
    head_ref[...] = ct_ref[...]

    @pl.when(pl.program_id(0) == pl.num_programs(0) - 1)
    def _():
        row = jnp.sum(acc_ref[...], axis=0, keepdims=True)
        for b in range(tokens // B):
            sq_ref[pl.ds(b, 1), :] = row[:, B * b : B * b + B]


def edge_kernel(nb, h_ref, sq_ref, out_ref):
    h = h_ref[...].astype(f32)
    part = jnp.sum(jnp.square(h).reshape(h.shape[0] // 8, 8, B), axis=0)
    edge = jnp.sum(part, axis=0, keepdims=True)
    rows = jnp.concatenate([edge, sq_ref[...], jnp.zeros((7, B), f32)], axis=0)
    for i in range(out_ref.shape[0]):
        out_ref[i] = rows


def inverse_rows(sq_ref, width):
    total = sq_ref[0]
    for i in range(1, sq_ref.shape[0]):
        total = total + sq_ref[i]
    return lax.rsqrt(total / width + eps_norm)


def grads_kernel(
    nb, ct_ref, ctn_ref, rate_ref, res_ref, four_ref, skip_ref, gml_ref, aft_ref, pack_ref
):
    step = pl.program_id(0)
    row, lane = iotas((B, B))
    upper = lane <= row
    back = ((B - lane) % B).astype(f32)
    below = row.astype(f32)
    slot = lane % 64
    first_half = lane < 64
    step_lane = lax.broadcasted_iota(jnp.int32, (16, B), 1)
    step_slot = step_lane % 64
    third = (step_slot >= 32) & (step_slot < 48)
    zeros = jnp.zeros((16, B), f32)
    none = jnp.zeros((16, B), bf16)
    rates = spread(rate_ref[pl.ds(step, 1), :])
    amps = spread(res_ref[pl.ds(step, 1), :]) * jnp.sqrt(2.0 * rates)
    reach = amps * jnp.exp(-rates * (float(B) - lane.astype(f32)))
    lags = amps * jnp.exp(-rates * back)
    skips = spread(skip_ref[pl.ds(step, 1), :])

    def near_part(g, fall):
        rows = pl.ds(16 * g, 16)
        sub = slice(16 * g, 16 * g + 16)
        blocks = [ct_ref[rows, pl.ds(B * b, B)] for b in range(nb)] + [ctn_ref[rows, :]]
        lhs = jnp.concatenate(blocks, axis=0)
        kernel_row = jnp.sum(lags[sub], axis=0, keepdims=True)
        toe = jnp.where(upper, toeplitz(kernel_row), 0.0)
        mine = jnp.where(first_half if g % 2 == 0 else ~first_half, fall, 0.0)
        hi, lo = split(jnp.concatenate([toe, mine], axis=1))
        out = mm(jnp.concatenate([lhs, lhs], axis=1), jnp.concatenate([hi, lo], axis=0), NN)
        direct = jnp.concatenate([skips[sub]] * (nb + 1), axis=0) * lhs.astype(f32)
        gml_ref[g] = out[:, :B] + direct
        return out[:, B:]

    def first_stage(p):
        pair_rates = four_ref[pl.ds(4 * step + p, 1), :]
        fall = jnp.exp(-pair_rates * below)
        fall = jnp.where((slot >= 16) & (slot < 32), fall * below, fall)
        return near_part(2 * p, fall) + near_part(2 * p + 1, fall), pair_rates

    def second_stage(p, states, pair_rates):
        decay = jnp.broadcast_to(jnp.exp(-pair_rates * float(B)), (16, B))
        after = zeros
        found = [after]
        for b in range(nb, 0, -1):
            state = states[16 * b : 16 * b + 16]
            state = jnp.where(third, state * float(B * b), state)
            after = state + decay * after
            found.append(after)
        after_all = jnp.concatenate(found[::-1], axis=0)
        aft_ref[p] = after_all
        one = after + pltpu.roll(after, B - 16, 1) - float(B) * pltpu.roll(after, 16, 1)
        tile = jnp.where(step_slot < 16, after, jnp.where(step_slot < 32, one, 0.0))
        tile = tile + pltpu.roll(tile, B - 32, 1)
        tile = jnp.where(step_lane < 64, tile, 0.0)
        a_hi, a_lo = split(after_all)
        halves = []
        for h in range(2):
            g = 2 * p + h
            g_hi, g_lo = split(reach[16 * g : 16 * g + 16])
            upper_rows = [g_hi, none, none, g_lo]
            lower_rows = [g_hi, none, none, none]
            gap = [none] * 4
            if h == 0:
                parts = upper_rows + gap + lower_rows + gap
            else:
                parts = gap + upper_rows + gap + lower_rows
            halves.append(jnp.concatenate(parts, axis=0))
        far = mm(
            jnp.concatenate([a_hi, a_lo], axis=1), jnp.concatenate(halves, axis=1), NN
        )
        gml_ref[2 * p] += far[:, :B]
        gml_ref[2 * p + 1] += far[:, B:]
        return tile

    held = first_stage(0)
    tiles = []
    for p in range(GB // 2):
        ahead = first_stage(p + 1) if p + 1 < GB // 2 else None
        tiles.append(second_stage(p, *held))
        held = ahead
    for k in range(GB // 4):
        pack_ref[k] = tiles[2 * k] + pltpu.roll(tiles[2 * k + 1], 64, 1)


def squeeze(tile):
    lane = lax.broadcasted_iota(jnp.int32, tile.shape, 1)
    tile = jnp.where(lane % 64 < 32, tile, 0.0)
    return jnp.where(lane < 64, tile + pltpu.roll(tile, B - 32, 1), 0.0)


def moments_kernel(
    nb, width, offset, h_ref, hp_ref, sq_ref, gain_ref, ct_ref, w_ref, rate_ref, four_ref,
    aft_ref, *refs,
):
    x_ref, part_ref, end_ref, w_scratch = refs[-4:]
    step = pl.program_id(0) + offset

    @pl.when(step == offset)
    def _():
        w_scratch[...] = w_ref[...].astype(f32)

    row, lane = iotas((B, B))
    upper = lane >= row
    ahead = lane.astype(f32)
    togo = float(B) - row.astype(f32)
    slot = lane % 64
    first_half = lane < 64
    step_slot = lax.broadcasted_iota(jnp.int32, (16, B), 1) % 64
    low = step_slot < 16
    half = step_slot < 32
    second = half & (step_slot >= 16)
    zeros = jnp.zeros((16, B), f32)
    inverse = inverse_rows(sq_ref, width)
    gains = spread(gain_ref[pl.ds(step, 1), :])

    def mix(g):
        rows = pl.ds(16 * g, 16)
        sub = slice(16 * g, 16 * g + 16)
        units = []
        for b in range(nb + 1):
            h = hp_ref[rows, :] if b == 0 else h_ref[rows, pl.ds(B * (b - 1), B)]
            units.append((h.astype(f32) * inverse[b : b + 1] * gains[sub]).astype(bf16))
        x_all = jnp.concatenate(units, axis=0)
        x_ref[g] = x_all
        lhs = jnp.concatenate([x_all[: 16 * nb], x_all[16:]], axis=1)
        taps = toeplitz(w_scratch[pl.ds(GB * step + g, 1), :])
        cur = jnp.where(upper, taps, 0.0).astype(bf16)
        prev = jnp.where(upper, 0.0, taps).astype(bf16)
        return mm(lhs, jnp.concatenate([prev, cur], axis=0), NN).astype(bf16)

    def first_stage(p):
        pair_rates = four_ref[pl.ds(4 * step + p, 1), :]
        rise = jnp.exp(-pair_rates * togo)
        rise = jnp.where(slot >= 48, rise * togo, rise)
        hi, lo = split(
            jnp.concatenate(
                [jnp.where(first_half, rise, 0.0), jnp.where(first_half, 0.0, rise)], axis=0
            )
        )
        mixes = [mix(2 * p), mix(2 * p + 1)]
        lifted = mm(
            jnp.concatenate(mixes, axis=1), jnp.concatenate([hi, lo], axis=1), NN
        )
        return mixes, lifted[:, :B] + lifted[:, B:], pair_rates

    skip_parts = []
    corrs = []

    def second_stage(p, mixes, lifted, pair_rates):
        for h in range(2):
            rows = pl.ds(16 * (2 * p + h), 16)
            mixed = mixes[h]
            ct = jnp.concatenate([ct_ref[rows, pl.ds(B * b, B)] for b in range(nb)], axis=0)
            pairs = mm(mixed, ct, TN)
            direct = ct.astype(f32) * mixed.astype(f32)
            total = direct[:16]
            for b in range(1, nb):
                total = total + direct[16 * b : 16 * b + 16]
            skip_parts.append(total)
            corrs.append(lag_sums(jnp.where(upper, pairs, 0.0)))
        after = aft_ref[p]
        decay = jnp.broadcast_to(jnp.exp(-pair_rates * float(B)), (16, B))
        plain = zeros
        scaled = zeros
        end = zeros
        for b in range(nb):
            lift = lifted[16 * b : 16 * b + 16]
            prod = lift * after[16 * b : 16 * b + 16]
            plain = plain + prod
            scaled = scaled + prod * float(B * (b + 1))
            end = decay * (end + jnp.where(second, lift * float(B * (nb - b)), lift))
        plain = plain[:8] + plain[8:]
        scaled = scaled[:8] + scaled[8:]
        after_one = (
            plain + pltpu.roll(plain, B - 16, 1) + pltpu.roll(plain, B - 32, 1)
            - pltpu.roll(scaled, 16, 1)
        )
        found = squeeze(jnp.where(low[:8], plain, after_one))
        ends_zero = squeeze(jnp.where(low, end, pltpu.roll(end, B - 16, 1)))
        ends_one = squeeze(
            jnp.where(low, pltpu.roll(end, B - 16, 1) + pltpu.roll(end, B - 48, 1), 0.0)
        )
        return found, ends_zero, ends_one

    held = first_stage(0)
    tiles = []
    for p in range(GB // 2):
        nxt = first_stage(p + 1) if p + 1 < GB // 2 else None
        tiles.append(second_stage(p, *held))
        held = nxt
    quads = []
    for k in range(GB // 4):
        left, right = tiles[2 * k], tiles[2 * k + 1]
        joined = [a + pltpu.roll(b, 64, 1) for a, b in zip(left, right)]
        quads.append(jnp.sum(joined[0], axis=0, keepdims=True))
        end_ref[k] = jnp.concatenate(joined[1:], axis=0)
    skip_row = lane_sums(jnp.concatenate(skip_parts, axis=0))
    corr = jnp.concatenate(corrs, axis=0)
    fall = jnp.exp(-spread(rate_ref[pl.ds(step, 1), :]) * ahead)
    table = []
    for g in range(GB):
        table += [fall[16 * g : 16 * g + 16], fall[16 * g : 16 * g + 16] * ahead[:16]]
    t_hi, t_lo = split(jnp.concatenate(table, axis=0))
    c_hi, c_lo = split(corr)
    near = mm(
        jnp.concatenate([c_hi, c_lo, c_hi], axis=1),
        jnp.concatenate([t_hi, t_hi, t_lo], axis=1),
        NT,
    )
    n_row, n_lane = iotas((GB, 32 * GB))
    near = jnp.sum(jnp.where(n_lane // 32 == n_row, near, 0.0), axis=0, keepdims=True)
    blank = jnp.zeros((1, B), f32)
    part_ref[...] = jnp.concatenate(
        [blank] * 6 + [skip_row] + [blank] * 3 + [quads[0] + near[:, :B]]
        + [blank] * 3 + [quads[1] + near[:, B:]] + [blank],
        axis=0,
    )


def mirror_matrix():
    row, lane = iotas((B, B))
    return jnp.where((row + lane) % B == 0, 1.0, 0.0).astype(bf16)


def inputs_kernel(
    nb, width, gml_ref, a_ref, rate_ref, res_ref, pair_ref, h_ref, sq_ref, gain_ref, w_ref,
    part_ref, end_ref, ig_ref, row_ref, pay_ref, grad_ref, acc_ref, w_scratch,
):
    step = pl.program_id(0)

    @pl.when(step == 0)
    def _():
        w_scratch[...] = mm(w_ref[...], mirror_matrix(), NN)
        acc_ref[...] = jnp.zeros_like(acc_ref)

    row, lane = iotas((B, B))
    upper = lane <= row
    none = jnp.zeros((16, B), bf16)
    ones = (lax.broadcasted_iota(jnp.int32, (16, B), 1) % 32) >= 16
    inverse = inverse_rows(sq_ref, width)
    gains = spread(gain_ref[pl.ds(step, 1), :])
    rates = spread(rate_ref[pl.ds(step, 1), :])
    amps = spread(res_ref[pl.ds(step, 1), :]) * jnp.sqrt(2.0 * rates)
    reach = amps * jnp.exp(-rates * (float(B) - lane.astype(f32)))
    sums = [acc_ref[pl.ds(8 * b, 8), :] for b in range(nb)]
    gain_parts = []
    quads = []
    lhs_of = {}

    def cross(k):
        decay = jnp.exp(jnp.broadcast_to(pair_ref[k], (16, B)) * (-float(B)))
        after = a_ref[k]
        ends = end_ref[k]
        first = jnp.sum(ends[:16] * after, axis=0, keepdims=True)
        other = jnp.sum(ends[16:] * after, axis=0, keepdims=True)
        quads.append(first + pltpu.roll(jnp.broadcast_to(other, (8, B)), 16, 1)[:1])
        after = jnp.where(ones, pltpu.roll(after, 16, 1), after)
        found = [after]
        for b in range(nb):
            after = after * decay
            found.append(after)
        a_hi, a_lo = split(jnp.concatenate(found[::-1], axis=0))
        return jnp.concatenate([a_hi, a_lo], axis=1)

    def first_stage(p):
        k = p // 2
        if k not in lhs_of:
            lhs_of[k] = cross(k)
        halves = []
        for h in range(2):
            g = 2 * p + h
            q = g % 4
            g_hi, g_lo = split(reach[16 * g : 16 * g + 16])
            pad = [none] * (2 * q)
            end = [none] * (6 - 2 * q)
            halves.append(
                jnp.concatenate(pad + [g_hi, g_lo] + end + pad + [g_hi, none] + end, axis=0)
            )
        far = mm(lhs_of[k], jnp.concatenate(halves, axis=1), NN)
        grads = []
        for h in range(2):
            g = 2 * p + h
            grad = (gml_ref[g] + far[:, B * h : B * h + B]).astype(bf16)
            grad_ref[g] = grad[: 16 * nb]
            grads.append(grad)
        return grads

    def second_stage(p, grads):
        for h in range(2):
            g = 2 * p + h
            rows = pl.ds(16 * g, 16)
            sub = slice(16 * g, 16 * g + 16)
            grad = grads[h]
            taps = toeplitz(w_scratch[pl.ds(GB * step + g, 1), :])
            cur = jnp.where(upper, taps, 0.0).astype(bf16)
            prev = jnp.where(upper, 0.0, taps).astype(bf16)
            lhs = jnp.concatenate([grad[: 16 * nb], grad[16:]], axis=1)
            ig = mm(lhs, jnp.concatenate([cur, prev], axis=0), NN)
            ig_ref[g] = ig
            part = jnp.zeros((16, B), f32)
            for b in range(nb):
                prod = ig[16 * b : 16 * b + 16] * h_ref[rows, pl.ds(B * b, B)].astype(f32)
                part = part + prod * inverse[b + 1 : b + 2]
                prod = prod * gains[sub]
                sums[b] = sums[b] + (prod[:8] + prod[8:])
            gain_parts.append(part)

    held = first_stage(0)
    for p in range(GB // 2):
        nxt = first_stage(p + 1) if p + 1 < GB // 2 else None
        second_stage(p, held)
        held = nxt
    for b in range(nb):
        acc_ref[pl.ds(8 * b, 8), :] = sums[b]
    gain_row = lane_sums(jnp.concatenate(gain_parts, axis=0))
    blank = jnp.zeros((1, B), f32)
    pay_ref[...] = part_ref[...] + jnp.concatenate(
        [blank, blank, gain_row] + [blank] * 7 + [quads[0]] + [blank] * 3 + [quads[1], blank],
        axis=0,
    )

    @pl.when(step == pl.num_programs(0) - 1)
    def _():
        raw = jnp.concatenate(
            [jnp.sum(sums[b], axis=0, keepdims=True) for b in range(nb)], axis=0
        )
        for i in range(row_ref.shape[0]):
            row_ref[i] = raw


def taps_kernel(nb, grad_ref, x_ref, pay_ref, out_ref, rows_ref):
    step = pl.program_id(0)
    steps = pl.num_programs(0)
    row, lane = iotas((B, B))
    lower = row >= lane

    def product(g):
        x_all = x_ref[g]
        x_pair = jnp.concatenate([x_all[16:], x_all[: 16 * nb]], axis=1)
        return mm(grad_ref[g], x_pair, TN)

    rows = []
    held = product(0)
    for g in range(GB):
        nxt = product(g + 1) if g + 1 < GB else None
        rows.append(lag_sums(jnp.where(lower, held[:, :B], held[:, B:])))
        held = nxt
    mirror = jnp.concatenate([mirror_matrix()] * 3, axis=0)
    taps = mm(fine(jnp.concatenate(rows, axis=0)), mirror, NN)
    rows_ref[pl.ds(pl.multiple_of(GB * step, GB), GB), :] = taps
    first = GB * 8
    for at, row in ((first + step, 2), (first + 8 + step, 6), (first + 16 + 2 * step, 10)):
        rows_ref[pl.ds(at, 1), :] = pay_ref[pl.ds(row, 1), :]
    rows_ref[pl.ds(first + 17 + 2 * step, 1), :] = pay_ref[pl.ds(14, 1), :]

    @pl.when(step == steps - 1)
    def _():
        rows = rows_ref[...]
        hi, lo = split(rows[first + 16 :])
        rows = jnp.concatenate([rows.astype(bf16), lo], axis=0)
        for i in range(out_ref.shape[0]):
            out_ref[i] = rows


def final_kernel(nb, width, ig_ref, h_ref, sq_ref, gain_ref, raw_ref, out_ref, rms_ref):
    step = pl.program_id(0)
    inverse = inverse_rows(sq_ref, width)
    gains = spread(gain_ref[pl.ds(step, 1), :])
    raw = raw_ref[0]
    for i in range(1, raw_ref.shape[0]):
        raw = raw + raw_ref[i]
    rms_ref[...] = raw * width ** (-0.5)
    inv = [inverse[b + 1 : b + 2] for b in range(nb)]
    pull = [raw[b : b + 1] * inv[b] * inv[b] * (1.0 / width) for b in range(nb)]
    for g in range(GB):
        rows = pl.ds(16 * g, 16)
        gain = gains[16 * g : 16 * g + 16]
        for b in range(nb):
            cols = pl.ds(B * b, B)
            h = h_ref[rows, cols].astype(f32)
            ig = ig_ref[g, pl.ds(16 * b, 16), :]
            out_ref[rows, cols] = (inv[b] * (ig * gain - h * pull[b])).astype(bf16)


def scan_kernel(count, span, s_ref, r_ref, out_ref):
    lane = lax.broadcasted_iota(jnp.int32, (8, B), 1)
    ones = (lane % 32) >= 16
    rates = r_ref[pl.ds(lax.axis_index("ctx") // 2, 1), :]
    decay = jnp.exp(jnp.broadcast_to(rates, (8, B)) * (-float(span)))
    x = jnp.zeros((8, B), f32)
    found = [None] * count
    found[count - 1] = x
    for i in range(count - 2, -1, -1):
        x = s_ref[i + 1] + decay * x
        found[i] = x
    v = jnp.zeros((8, B), f32)
    out_ref[count - 1] = v
    for i in range(count - 2, -1, -1):
        v = decay * (v + float(span) * pltpu.roll(found[i + 1], 16, 1))
        out_ref[i] = found[i] + jnp.where(ones, v, 0.0)


def outs_kernel(scale, in_ref, tap_ref, gain_ref, skip_ref, mom_ref):
    total = in_ref[0].astype(f32)
    for i in range(1, in_ref.shape[0]):
        total = total + in_ref[i].astype(f32)
    total = total * scale
    start = 0
    for ref in (tap_ref, gain_ref, skip_ref, mom_ref):
        size = ref.shape[0]
        ref[...] = total[start : start + size]
        start += size
    mom_ref[...] += total[start:]


def call(kernel, name, grid, ins, outs, args, flops=0, moved=0, scratch=(), aliases={}):
    return pl.pallas_call(
        kernel,
        name=name,
        grid=grid,
        in_specs=ins,
        out_specs=outs[0],
        out_shape=outs[1],
        scratch_shapes=scratch,
        input_output_aliases=aliases,
        compiler_params=pltpu.CompilerParams(vmem_limit_bytes=VMEM),
        cost_estimate=pl.CostEstimate(flops=flops, bytes_accessed=moved, transcendentals=0),
    )(*args)


def in_hbm(*arrays):
    return tuple(pltpu.with_memory_space_constraint(x, pltpu.HBM) for x in arrays)


def exchange(x, axis):
    return lax.all_to_all(x, axis, 0, 0, tiled=True)


def local(hidden, cotangent, norm_gain, mr_filter, residue, decay_rate, skip_weight):
    channels, tokens = hidden.shape
    groups, taps = mr_filter.shape
    modes = residue.shape[1]
    n_ctx = lax.axis_size("ctx")
    n_ch = lax.axis_size("ch")
    width = channels * n_ch
    scale = (tokens * n_ctx) ** (-0.5)
    nb = tokens // B
    steps = groups // GB
    grid = (steps,)
    shape = jax.ShapeDtypeStruct
    hidden, cotangent, mr_filter = in_hbm(hidden, cotangent, mr_filter)

    wide = pl.BlockSpec((16 * GB, tokens), lambda i: (i, 0))
    thin = pl.BlockSpec((16 * GB, B), lambda i: (i, 0))
    tall = pl.BlockSpec((GB, 16 * (nb + 1), B), lambda i: (i, 0, 0))
    pair_tall = pl.BlockSpec((GB // 2, 16 * (nb + 1), B), lambda i: (i, 0, 0))
    body = pl.BlockSpec((GB, 16 * nb, B), lambda i: (i, 0, 0))
    quad = pl.BlockSpec((GB // 4, 16, B), lambda i: (i, 0, 0))
    quad_two = pl.BlockSpec((GB // 4, 32, B), lambda i: (i, 0, 0))
    quad_row = pl.BlockSpec((GB // 4, 1, B), lambda i: (i, 0, 0))
    pay = pl.BlockSpec((16, B), lambda i: (i, 0))

    def full(*dims):
        return pl.BlockSpec(dims, lambda *i: (0,) * len(dims))

    tail, head, own_sq = call(
        prep_kernel,
        "prep",
        grid,
        [wide, thin],
        (
            [thin, thin, full(nb, B)],
            [shape((channels, B), bf16), shape((channels, B), bf16), shape((nb, B), f32)],
        ),
        (hidden, cotangent),
        moved=3 * 2**20,
        scratch=[pltpu.VMEM((8, tokens), f32)],
    )
    ct_next = lax.ppermute(head, "ctx", [(i, i - 1) for i in range(1, n_ctx)])
    h_prev = lax.ppermute(tail, "ctx", [(i, i + 1) for i in range(n_ctx - 1)])
    edge = call(
        functools.partial(edge_kernel, nb),
        "edge",
        (),
        [full(channels, B), full(nb, B)],
        (full(n_ch, 16, B), shape((n_ch, 16, B), f32)),
        (h_prev, own_sq),
        moved=2**18,
    )
    edge, ct_next = lax.optimization_barrier((edge, ct_next))
    squares = exchange(edge, "ch")

    rate_flat = decay_rate.reshape(steps, B)
    res_flat = residue.reshape(steps, B)
    rate_four = jnp.tile(decay_rate, (1, 4)).reshape(groups // 2, B)
    rate_pair = jnp.concatenate([decay_rate, decay_rate], axis=1).reshape(groups // 4, B)
    gain_flat = norm_gain.reshape(steps, B)
    skip_flat = skip_weight.reshape(steps, B)
    flat = full(steps, B)

    grad_local, after_local, packed = call(
        functools.partial(grads_kernel, nb),
        "grads",
        grid,
        [wide, thin, flat, flat, full(groups // 2, B), flat],
        (
            [tall, pair_tall, quad],
            [
                pltpu.HBM((groups, 16 * (nb + 1), B), f32),
                pltpu.HBM((groups // 2, 16 * (nb + 1), B), f32),
                shape((groups // 4, 16, B), f32),
            ],
        ),
        (cotangent, ct_next, rate_flat, res_flat, rate_four, skip_flat),
        flops=groups * 2 * 144 * 256 * 384,
        moved=14 * 2**20,
    )

    def moments(offset, before, x_next):
        def at(spec):
            return pl.BlockSpec(
                spec.block_shape, lambda i: (i + offset,) + spec.index_map(i)[1:]
            )

        held = [pl.BlockSpec(memory_space=pl.ANY)] * len(before)
        return call(
            functools.partial(moments_kernel, nb, width, offset),
            "moments",
            (steps // 2,),
            [
                at(wide), at(thin), full(n_ch, 16, B), flat, at(wide), full(groups, B), flat,
                full(groups // 2, B), at(pair_tall),
            ]
            + held,
            (
                [at(tall), at(pay), at(quad_two)],
                [
                    pltpu.HBM((groups, 16 * (nb + 1), B), bf16),
                    shape((16 * steps, B), f32),
                    shape((groups // 4, 32, B), f32),
                ],
            ),
            (
                hidden, x_next, squares, gain_flat, cotangent, mr_filter, rate_flat, rate_four,
                after_local, *before,
            ),
            flops=groups * 128 * 256 * 384,
            moved=7 * 2**20,
            scratch=[pltpu.VMEM((groups, B), f32)],
            aliases={9 + i: i for i in range(len(before))},
        )

    grad_local, after_local = in_hbm(grad_local, after_local)
    arrived = exchange(packed.reshape(n_ctx, 8, B), "ctx")
    early = moments(0, (), h_prev)
    early = in_hbm(early[0]) + tuple(early[1:])
    arrived, early = lax.optimization_barrier((arrived, tuple(early)))
    scanned = call(
        functools.partial(scan_kernel, n_ctx, tokens),
        "scan",
        (),
        [full(n_ctx, 8, B), full(groups // 4, B)],
        (full(n_ctx, 8, B), shape((n_ctx, 8, B), f32)),
        (arrived, rate_pair),
        moved=2**18,
    )
    scanned, edge_rows = lax.optimization_barrier((scanned, h_prev))
    after = exchange(scanned, "ctx").reshape(groups // 4, 16, B)
    units, part, ends = moments(steps // 2, early, edge_rows)
    (units,) = in_hbm(units)

    ig, row_part, mostly, grad_mixed = call(
        functools.partial(inputs_kernel, nb, width),
        "inputs",
        grid,
        [
            tall, quad, flat, flat, quad_row, wide, full(n_ch, 16, B), flat, full(groups, B),
            pay, quad_two,
        ],
        (
            [body, full(n_ch, nb, B), pay, body],
            [
                pltpu.HBM((groups, 16 * nb, B), f32),
                shape((n_ch, nb, B), f32),
                shape((16 * steps, B), f32),
                pltpu.HBM((groups, 16 * nb, B), bf16),
            ],
        ),
        (
            grad_local, after, rate_flat, res_flat, rate_pair.reshape(groups // 4, 1, B), hidden,
            squares, gain_flat, mr_filter, part, ends,
        ),
        flops=groups * 2 * 144 * 256 * 512,
        moved=14 * 2**20,
        scratch=[pltpu.VMEM((8 * nb, B), f32), pltpu.VMEM((groups, B), f32)],
    )

    ig, grad_mixed = in_hbm(ig, grad_mixed)
    raw = exchange(row_part, "ch")
    extra = groups // 4
    lines = groups + 2 * steps + 2 * extra
    payload = call(
        functools.partial(taps_kernel, nb),
        "taps",
        grid,
        [body, tall, pay],
        (full(n_ctx, lines, B), shape((n_ctx, lines, B), bf16)),
        (grad_mixed, units, mostly),
        flops=groups * 2 * 128 * 128 * 256,
        moved=5 * 2**20,
        scratch=[pltpu.VMEM((lines - extra, B), f32)],
    )
    raw, payload = lax.optimization_barrier((raw, payload))
    landed = exchange(payload, "ctx")
    grad_hidden, grad_inv_rms = call(
        functools.partial(final_kernel, nb, width),
        "final",
        grid,
        [body, wide, full(n_ch, 16, B), flat, full(n_ch, nb, B)],
        (
            [wide, full(nb, B)],
            [shape((channels, tokens), bf16), shape((nb, B), f32)],
        ),
        (ig, hidden, squares, gain_flat, raw),
        moved=8 * 2**20,
    )
    landed, grad_inv_rms = lax.optimization_barrier((landed, grad_inv_rms))
    grad_mr, grad_gain, grad_skip, both = call(
        functools.partial(outs_kernel, scale),
        "outs",
        (),
        [full(n_ctx, lines, B)],
        (
            [full(groups, taps), full(steps, B), full(steps, B), full(groups // 4, B)],
            [
                shape((groups, taps), f32),
                shape((steps, B), f32),
                shape((steps, B), f32),
                shape((groups // 4, B), f32),
            ],
        ),
        (landed,),
        moved=2**20,
    )
    both = both.reshape(groups, 2 * modes)
    first, second = both[:, :modes], both[:, modes:]
    root_rate = jnp.sqrt(2.0 * decay_rate)
    return (
        grad_hidden,
        grad_gain.reshape(channels),
        grad_mr,
        root_rate * first,
        residue * root_rate * (0.5 * first - decay_rate * second),
        grad_skip.reshape(channels),
        grad_inv_rms.reshape(tokens),
    )


def solution(mesh):
    return jax.shard_map(
        local,
        mesh=mesh,
        in_specs=(
            P("ch", "ctx"),
            P("ch", "ctx"),
            P("ch"),
            P("ch", None),
            P("ch", None),
            P("ch", None),
            P("ch"),
        ),
        out_specs=(
            P("ch", "ctx"),
            P("ch"),
            P("ch", None),
            P("ch", None),
            P("ch", None),
            P("ch"),
            P("ctx"),
        ),
        check_vma=False,
    )
```

```python
import functools

import jax
import jax.numpy as jnp
from jax import lax
from jax.experimental import pallas as pl
from jax.experimental.pallas import tpu as pltpu
from jax.sharding import PartitionSpec as P

eps_norm = 1e-06
B = 128
GB = 8
VMEM = 30 * 1024 * 1024
PER = {"prep": 4, "grads": 2, "moments": 1, "inputs": 4, "taps": 2, "final": 4}
f32 = jnp.float32
bf16 = jnp.bfloat16

NN = (((1,), (0,)), ((), ()))
NT = (((1,), (1,)), ((), ()))
TN = (((0,), (0,)), ((), ()))


def mm(a, b, dims):
    return lax.dot_general(a, b, dims, preferred_element_type=f32)


def split(x):
    hi = x.astype(bf16)
    lo = (x - hi.astype(f32)).astype(bf16)
    return hi, lo


def iotas(shape):
    return (
        lax.broadcasted_iota(jnp.int32, shape, 0),
        lax.broadcasted_iota(jnp.int32, shape, 1),
    )


def spread(row):
    return jnp.transpose(jnp.broadcast_to(row, (B, B)))


def fine(x):
    hi, mid = split(x)
    low = (x - hi.astype(f32) - mid.astype(f32)).astype(bf16)
    return jnp.concatenate([hi, mid, low], axis=1)


def lane_sums(x):
    return mm(jnp.ones((8, 3 * B), bf16), fine(x), NT)[:1]


def turned_sums(x):
    return jnp.sum(jnp.transpose(x), axis=0, keepdims=True)


def toeplitz(row):
    full = jnp.broadcast_to(row, (B, B))
    return pltpu.roll(full, 0, 1, stride=1, stride_axis=0)


def lag_sums(square):
    total = square[:8]
    for a in range(8, B, 8):
        total = total + pltpu.roll(square[a : a + 8], B - a, 1)
    row = lax.broadcasted_iota(jnp.int32, (8, B), 0)
    for bit in (1, 2, 4):
        total = jnp.where((row & bit) != 0, pltpu.roll(total, B - bit, 1), total)
    return jnp.sum(total, axis=0, keepdims=True)


def prep_kernel(at, h_ref, ct_ref, tail_ref, head_ref, sq_ref, acc_ref):
    tokens = h_ref.shape[1]

    def clear():
        acc_ref[...] = jnp.zeros_like(acc_ref)

    begin(at, clear)
    h = h_ref[...].astype(f32)
    acc_ref[...] += jnp.sum(jnp.square(h).reshape(h.shape[0] // 8, 8, tokens), axis=0)
    tail_ref[...] = h_ref[:, tokens - B :]
    head_ref[...] = ct_ref[...]

    def write():
        row = jnp.sum(acc_ref[...], axis=0, keepdims=True)
        for b in range(tokens // B):
            sq_ref[pl.ds(b, 1), :] = row[:, B * b : B * b + B]

    finish(at, write)


def edge_kernel(nb, h_ref, sq_ref, out_ref):
    h = h_ref[...].astype(f32)
    part = jnp.sum(jnp.square(h).reshape(h.shape[0] // 8, 8, B), axis=0)
    edge = jnp.sum(part, axis=0, keepdims=True)
    rows = jnp.concatenate([edge, sq_ref[...], jnp.zeros((7, B), f32)], axis=0)
    for i in range(out_ref.shape[0]):
        out_ref[i] = rows


def inverse_rows(sq_ref, width):
    total = sq_ref[0]
    for i in range(1, sq_ref.shape[0]):
        total = total + sq_ref[i]
    return lax.rsqrt(total / width + eps_norm)


def grads_kernel(
    nb, at, ct_ref, ctn_ref, rate_ref, res_ref, four_ref, skip_ref, gml_ref, aft_ref, pack_ref
):
    step = at[0]
    row, lane = iotas((B, B))
    upper = lane <= row
    back = ((B - lane) % B).astype(f32)
    below = row.astype(f32)
    slot = lane % 64
    first_half = lane < 64
    step_lane = lax.broadcasted_iota(jnp.int32, (16, B), 1)
    step_slot = step_lane % 64
    third = (step_slot >= 32) & (step_slot < 48)
    zeros = jnp.zeros((16, B), f32)
    none = jnp.zeros((16, B), bf16)
    rates = spread(rate_ref[pl.ds(step, 1), :])
    amps = spread(res_ref[pl.ds(step, 1), :]) * jnp.sqrt(2.0 * rates)
    reach = amps * jnp.exp(-rates * (float(B) - lane.astype(f32)))
    lags = amps * jnp.exp(-rates * back)
    skips = spread(skip_ref[pl.ds(step, 1), :])

    def near_part(g, fall):
        rows = pl.ds(16 * g, 16)
        sub = slice(16 * g, 16 * g + 16)
        blocks = [ct_ref[rows, pl.ds(B * b, B)] for b in range(nb)] + [ctn_ref[rows, :]]
        lhs = jnp.concatenate(blocks, axis=0)
        kernel_row = jnp.sum(lags[sub], axis=0, keepdims=True)
        toe = jnp.where(upper, toeplitz(kernel_row), 0.0)
        mine = jnp.where(first_half if g % 2 == 0 else ~first_half, fall, 0.0)
        hi, lo = split(jnp.concatenate([toe, mine], axis=1))
        out = mm(jnp.concatenate([lhs, lhs], axis=1), jnp.concatenate([hi, lo], axis=0), NN)
        direct = jnp.concatenate([skips[sub]] * (nb + 1), axis=0) * lhs.astype(f32)
        gml_ref[g] = out[:, :B] + direct
        return out[:, B:]

    def first_stage(p):
        pair_rates = four_ref[pl.ds(4 * step + p, 1), :]
        fall = jnp.exp(-pair_rates * below)
        fall = jnp.where((slot >= 16) & (slot < 32), fall * below, fall)
        return near_part(2 * p, fall) + near_part(2 * p + 1, fall), pair_rates

    def second_stage(p, states, pair_rates):
        decay = jnp.broadcast_to(jnp.exp(-pair_rates * float(B)), (16, B))
        after = zeros
        found = [after]
        for b in range(nb, 0, -1):
            state = states[16 * b : 16 * b + 16]
            state = jnp.where(third, state * float(B * b), state)
            after = state + decay * after
            found.append(after)
        after_all = jnp.concatenate(found[::-1], axis=0)
        aft_ref[p] = after_all
        one = after + pltpu.roll(after, B - 16, 1) - float(B) * pltpu.roll(after, 16, 1)
        tile = jnp.where(step_slot < 16, after, jnp.where(step_slot < 32, one, 0.0))
        tile = tile + pltpu.roll(tile, B - 32, 1)
        tile = jnp.where(step_lane < 64, tile, 0.0)
        a_hi, a_lo = split(after_all)
        halves = []
        for h in range(2):
            g = 2 * p + h
            g_hi, g_lo = split(reach[16 * g : 16 * g + 16])
            upper_rows = [g_hi, none, none, g_lo]
            lower_rows = [g_hi, none, none, none]
            gap = [none] * 4
            if h == 0:
                parts = upper_rows + gap + lower_rows + gap
            else:
                parts = gap + upper_rows + gap + lower_rows
            halves.append(jnp.concatenate(parts, axis=0))
        far = mm(
            jnp.concatenate([a_hi, a_lo], axis=1), jnp.concatenate(halves, axis=1), NN
        )
        gml_ref[2 * p] += far[:, :B]
        gml_ref[2 * p + 1] += far[:, B:]
        return tile

    held = first_stage(0)
    tiles = []
    for p in range(GB // 2):
        ahead = first_stage(p + 1) if p + 1 < GB // 2 else None
        tiles.append(second_stage(p, *held))
        held = ahead
    for k in range(GB // 4):
        pack_ref[k] = tiles[2 * k] + pltpu.roll(tiles[2 * k + 1], 64, 1)


def squeeze(tile):
    lane = lax.broadcasted_iota(jnp.int32, tile.shape, 1)
    tile = jnp.where(lane % 64 < 32, tile, 0.0)
    return jnp.where(lane < 64, tile + pltpu.roll(tile, B - 32, 1), 0.0)


def moments_kernel(
    nb, width, at, h_ref, hp_ref, sq_ref, gain_ref, ct_ref, w_ref, pair_ref, four_ref,
    aft_ref, *refs,
):
    x_ref, part_ref, end_ref, w_scratch = refs[-4:]
    step = at[0]

    def load():
        w_scratch[...] = w_ref[...].astype(f32)

    begin(at, load)

    row, lane = iotas((B, B))
    upper = lane >= row
    togo = float(B) - row.astype(f32)
    slot = lane % 64
    first_half = lane < 64
    step_slot = lax.broadcasted_iota(jnp.int32, (16, B), 1) % 64
    low = step_slot < 16
    half = step_slot < 32
    second = half & (step_slot >= 16)
    zeros = jnp.zeros((16, B), f32)
    inverse = inverse_rows(sq_ref, width)
    gains = spread(gain_ref[pl.ds(step, 1), :])

    def mix(g):
        rows = pl.ds(16 * g, 16)
        sub = slice(16 * g, 16 * g + 16)
        units = []
        for b in range(nb + 1):
            h = hp_ref[rows, :] if b == 0 else h_ref[rows, pl.ds(B * (b - 1), B)]
            units.append((h.astype(f32) * inverse[b : b + 1] * gains[sub]).astype(bf16))
        x_all = jnp.concatenate(units, axis=0)
        x_ref[g] = x_all
        lhs = jnp.concatenate([x_all[: 16 * nb], x_all[16:]], axis=1)
        taps = toeplitz(w_scratch[pl.ds(GB * step + g, 1), :])
        cur = jnp.where(upper, taps, 0.0).astype(bf16)
        prev = jnp.where(upper, 0.0, taps).astype(bf16)
        return mm(lhs, jnp.concatenate([prev, cur], axis=0), NN).astype(bf16)

    def first_stage(p):
        pair_rates = four_ref[pl.ds(4 * step + p, 1), :]
        rise = jnp.exp(-pair_rates * togo)
        rise = jnp.where(slot >= 48, rise * togo, rise)
        hi, lo = split(
            jnp.concatenate(
                [jnp.where(first_half, rise, 0.0), jnp.where(first_half, 0.0, rise)], axis=0
            )
        )
        mixes = [mix(2 * p), mix(2 * p + 1)]
        lifted = mm(
            jnp.concatenate(mixes, axis=1), jnp.concatenate([hi, lo], axis=1), NN
        )
        return mixes, lifted[:, :B] + lifted[:, B:], pair_rates

    skip_parts = []
    corrs = []

    def second_stage(p, mixes, lifted, pair_rates):
        for h in range(2):
            rows = pl.ds(16 * (2 * p + h), 16)
            mixed = mixes[h]
            ct = jnp.concatenate([ct_ref[rows, pl.ds(B * b, B)] for b in range(nb)], axis=0)
            pairs = mm(mixed, ct, TN)
            direct = ct.astype(f32) * mixed.astype(f32)
            total = direct[:16]
            for b in range(1, nb):
                total = total + direct[16 * b : 16 * b + 16]
            skip_parts.append(total)
            corrs.append(lag_sums(jnp.where(upper, pairs, 0.0)))
        after = aft_ref[p]
        decay = jnp.broadcast_to(jnp.exp(-pair_rates * float(B)), (16, B))
        plain = zeros
        scaled = zeros
        end = zeros
        for b in range(nb):
            lift = lifted[16 * b : 16 * b + 16]
            prod = lift * after[16 * b : 16 * b + 16]
            plain = plain + prod
            scaled = scaled + prod * float(B * (b + 1))
            end = decay * (end + jnp.where(second, lift * float(B * (nb - b)), lift))
        plain = plain[:8] + plain[8:]
        scaled = scaled[:8] + scaled[8:]
        after_one = (
            plain + pltpu.roll(plain, B - 16, 1) + pltpu.roll(plain, B - 32, 1)
            - pltpu.roll(scaled, 16, 1)
        )
        found = squeeze(jnp.where(low[:8], plain, after_one))
        ends_zero = squeeze(jnp.where(low, end, pltpu.roll(end, B - 16, 1)))
        ends_one = squeeze(
            jnp.where(low, pltpu.roll(end, B - 16, 1) + pltpu.roll(end, B - 48, 1), 0.0)
        )
        return found, ends_zero, ends_one

    held = first_stage(0)
    tiles = []
    for p in range(GB // 2):
        nxt = first_stage(p + 1) if p + 1 < GB // 2 else None
        tiles.append(second_stage(p, *held))
        held = nxt
    quads = []
    for k in range(GB // 4):
        left, right = tiles[2 * k], tiles[2 * k + 1]
        joined = [a + pltpu.roll(b, 64, 1) for a, b in zip(left, right)]
        quads.append(jnp.sum(joined[0], axis=0, keepdims=True))
        end_ref[k] = jnp.concatenate(joined[1:], axis=0)
    skip_row = lane_sums(jnp.concatenate(skip_parts, axis=0))
    below = row.astype(f32)
    tables = []
    for k in range(GB // 4):
        fall = jnp.exp(-jnp.broadcast_to(pair_ref[k], (B, B)) * below)
        tables.append(jnp.where(lane % 32 < 16, fall, fall * below))
    t_hi, t_lo = split(jnp.concatenate(tables, axis=1))
    c_hi, c_lo = split(jnp.concatenate(corrs, axis=0))
    near = mm(
        jnp.concatenate([c_hi, c_lo, c_hi], axis=1),
        jnp.concatenate([t_hi, t_hi, t_lo], axis=0),
        NN,
    )
    n_row, n_lane = iotas((GB, 32 * GB))
    near = jnp.sum(jnp.where(n_lane // 32 == n_row, near, 0.0), axis=0, keepdims=True)
    blank = jnp.zeros((1, B), f32)
    part_ref[...] = jnp.concatenate(
        [blank] * 6 + [skip_row] + [blank] * 3 + [quads[0] + near[:, :B]]
        + [blank] * 3 + [quads[1] + near[:, B:]] + [blank],
        axis=0,
    )


def mirror_matrix():
    row, lane = iotas((B, B))
    return jnp.where((row + lane) % B == 0, 1.0, 0.0).astype(bf16)


def inputs_kernel(
    nb, width, at, gml_ref, a_ref, rate_ref, res_ref, pair_ref, h_ref, sq_ref, gain_ref, w_ref,
    part_ref, end_ref, ig_ref, row_ref, pay_ref, grad_ref, acc_ref, w_scratch,
):
    step = at[0]

    def load():
        w_scratch[...] = mm(w_ref[...], mirror_matrix(), NN)
        acc_ref[...] = jnp.zeros_like(acc_ref)

    begin(at, load)

    row, lane = iotas((B, B))
    upper = lane <= row
    none = jnp.zeros((16, B), bf16)
    ones = (lax.broadcasted_iota(jnp.int32, (16, B), 1) % 32) >= 16
    inverse = inverse_rows(sq_ref, width)
    gains = spread(gain_ref[pl.ds(step, 1), :])
    rates = spread(rate_ref[pl.ds(step, 1), :])
    amps = spread(res_ref[pl.ds(step, 1), :]) * jnp.sqrt(2.0 * rates)
    reach = amps * jnp.exp(-rates * (float(B) - lane.astype(f32)))
    sums = [acc_ref[pl.ds(8 * b, 8), :] for b in range(nb)]
    gain_parts = []
    quads = []
    lhs_of = {}

    def cross(k):
        decay = jnp.exp(jnp.broadcast_to(pair_ref[k], (16, B)) * (-float(B)))
        after = a_ref[k]
        ends = end_ref[k]
        first = jnp.sum(ends[:16] * after, axis=0, keepdims=True)
        other = jnp.sum(ends[16:] * after, axis=0, keepdims=True)
        quads.append(first + pltpu.roll(jnp.broadcast_to(other, (8, B)), 16, 1)[:1])
        after = jnp.where(ones, pltpu.roll(after, 16, 1), after)
        found = [after]
        for b in range(nb):
            after = after * decay
            found.append(after)
        a_hi, a_lo = split(jnp.concatenate(found[::-1], axis=0))
        return jnp.concatenate([a_hi, a_lo], axis=1)

    def first_stage(p):
        k = p // 2
        if k not in lhs_of:
            lhs_of[k] = cross(k)
        halves = []
        for h in range(2):
            g = 2 * p + h
            q = g % 4
            g_hi, g_lo = split(reach[16 * g : 16 * g + 16])
            pad = [none] * (2 * q)
            end = [none] * (6 - 2 * q)
            halves.append(
                jnp.concatenate(pad + [g_hi, g_lo] + end + pad + [g_hi, none] + end, axis=0)
            )
        far = mm(lhs_of[k], jnp.concatenate(halves, axis=1), NN)
        grads = []
        for h in range(2):
            g = 2 * p + h
            grad = (gml_ref[g] + far[:, B * h : B * h + B]).astype(bf16)
            grad_ref[g] = grad[: 16 * nb]
            grads.append(grad)
        return grads

    def second_stage(p, grads):
        for h in range(2):
            g = 2 * p + h
            rows = pl.ds(16 * g, 16)
            sub = slice(16 * g, 16 * g + 16)
            grad = grads[h]
            taps = toeplitz(w_scratch[pl.ds(GB * step + g, 1), :])
            cur = jnp.where(upper, taps, 0.0).astype(bf16)
            prev = jnp.where(upper, 0.0, taps).astype(bf16)
            lhs = jnp.concatenate([grad[: 16 * nb], grad[16:]], axis=1)
            ig = mm(lhs, jnp.concatenate([cur, prev], axis=0), NN)
            ig_ref[g] = ig
            part = jnp.zeros((16, B), f32)
            for b in range(nb):
                prod = ig[16 * b : 16 * b + 16] * h_ref[rows, pl.ds(B * b, B)].astype(f32)
                part = part + prod * inverse[b + 1 : b + 2]
                prod = prod * gains[sub]
                sums[b] = sums[b] + (prod[:8] + prod[8:])
            gain_parts.append(part)

    held = first_stage(0)
    for p in range(GB // 2):
        nxt = first_stage(p + 1) if p + 1 < GB // 2 else None
        second_stage(p, held)
        held = nxt
    for b in range(nb):
        acc_ref[pl.ds(8 * b, 8), :] = sums[b]
    gain_row = turned_sums(jnp.concatenate(gain_parts, axis=0))
    blank = jnp.zeros((1, B), f32)
    pay_ref[...] = part_ref[...] + jnp.concatenate(
        [blank, blank, gain_row] + [blank] * 7 + [quads[0]] + [blank] * 3 + [quads[1], blank],
        axis=0,
    )

    def write():
        raw = jnp.concatenate(
            [jnp.sum(sums[b], axis=0, keepdims=True) for b in range(nb)], axis=0
        )
        for i in range(row_ref.shape[0]):
            row_ref[i] = raw

    finish(at, write)


def taps_kernel(nb, at, grad_ref, x_ref, pay_ref, out_ref, rows_ref):
    step = at[0]
    row, lane = iotas((B, B))
    lower = row >= lane

    def product(g):
        x_all = x_ref[g]
        x_pair = jnp.concatenate([x_all[16:], x_all[: 16 * nb]], axis=1)
        return mm(grad_ref[g], x_pair, TN)

    rows = []
    held = product(0)
    for g in range(GB):
        nxt = product(g + 1) if g + 1 < GB else None
        rows.append(lag_sums(jnp.where(lower, held[:, :B], held[:, B:])))
        held = nxt
    mirror = jnp.concatenate([mirror_matrix()] * 3, axis=0)
    taps = mm(fine(jnp.concatenate(rows, axis=0)), mirror, NN)
    rows_ref[pl.ds(pl.multiple_of(GB * step, GB), GB), :] = taps
    first = GB * 8
    for line, row in ((first + step, 2), (first + 8 + step, 6), (first + 16 + 2 * step, 10)):
        rows_ref[pl.ds(line, 1), :] = pay_ref[pl.ds(row, 1), :]
    rows_ref[pl.ds(first + 17 + 2 * step, 1), :] = pay_ref[pl.ds(14, 1), :]

    def write():
        rows = rows_ref[...]
        hi, lo = split(rows[first + 16 :])
        rows = jnp.concatenate([rows.astype(bf16), lo], axis=0)
        for i in range(out_ref.shape[0]):
            out_ref[i] = rows

    finish(at, write)


def final_kernel(nb, width, at, ig_ref, h_ref, sq_ref, gain_ref, raw_ref, out_ref, rms_ref):
    step = at[0]
    inverse = inverse_rows(sq_ref, width)
    gains = spread(gain_ref[pl.ds(step, 1), :])
    raw = raw_ref[0]
    for i in range(1, raw_ref.shape[0]):
        raw = raw + raw_ref[i]
    rms_ref[...] = raw * width ** (-0.5)
    inv = [inverse[b + 1 : b + 2] for b in range(nb)]
    pull = [raw[b : b + 1] * inv[b] * inv[b] * (1.0 / width) for b in range(nb)]
    for g in range(GB):
        rows = pl.ds(16 * g, 16)
        gain = gains[16 * g : 16 * g + 16]
        for b in range(nb):
            cols = pl.ds(B * b, B)
            h = h_ref[rows, cols].astype(f32)
            ig = ig_ref[g, pl.ds(16 * b, 16), :]
            out_ref[rows, cols] = (inv[b] * (ig * gain - h * pull[b])).astype(bf16)


def scan_kernel(count, span, s_ref, r_ref, out_ref):
    lane = lax.broadcasted_iota(jnp.int32, (8, B), 1)
    ones = (lane % 32) >= 16
    rates = r_ref[pl.ds(lax.axis_index("ctx") // 2, 1), :]
    decay = jnp.exp(jnp.broadcast_to(rates, (8, B)) * (-float(span)))
    x = jnp.zeros((8, B), f32)
    found = [None] * count
    found[count - 1] = x
    for i in range(count - 2, -1, -1):
        x = s_ref[i + 1] + decay * x
        found[i] = x
    v = jnp.zeros((8, B), f32)
    out_ref[count - 1] = v
    for i in range(count - 2, -1, -1):
        v = decay * (v + float(span) * pltpu.roll(found[i + 1], 16, 1))
        out_ref[i] = found[i] + jnp.where(ones, v, 0.0)


def outs_kernel(scale, in_ref, tap_ref, gain_ref, skip_ref, mom_ref):
    total = in_ref[0].astype(f32)
    for i in range(1, in_ref.shape[0]):
        total = total + in_ref[i].astype(f32)
    total = total * scale
    start = 0
    for ref in (tap_ref, gain_ref, skip_ref, mom_ref):
        size = ref.shape[0]
        ref[...] = total[start : start + size]
        start += size
    mom_ref[...] += total[start:]


def call(
    kernel, name, ins, outs, args, steps=0, per=1, offset=0, flops=0, moved=0, scratch=(),
    aliases={},
):
    def spec(entry):
        if isinstance(entry, pl.BlockSpec):
            return entry
        lead, rest = entry[0], tuple(entry[1:])
        if lead is None:
            return pl.BlockSpec(rest, lambda *i: (0,) * len(rest))
        return pl.BlockSpec(
            (lead * per,) + rest, lambda i: (i + offset // per,) + (0,) * len(rest)
        )

    entries = list(ins) + list(outs[0]) + [(None,)] * len(scratch)

    def body(*refs):
        if not steps:
            kernel(*refs)
            return
        for sub in range(per):
            views = []
            for entry, ref in zip(entries, refs):
                if isinstance(entry, pl.BlockSpec) or entry[0] is None or per == 1:
                    views.append(ref)
                else:
                    views.append(ref.at[pl.ds(sub * entry[0], entry[0])])
            kernel((pl.program_id(0) * per + sub + offset, sub == 0, sub == per - 1), *views)

    return pl.pallas_call(
        body,
        name=name,
        grid=(steps // per,) if steps else (),
        in_specs=[spec(entry) for entry in ins],
        out_specs=[spec(entry) for entry in outs[0]],
        out_shape=list(outs[1]),
        scratch_shapes=scratch,
        input_output_aliases=aliases,
        compiler_params=pltpu.CompilerParams(vmem_limit_bytes=VMEM),
        cost_estimate=pl.CostEstimate(flops=flops, bytes_accessed=moved, transcendentals=0),
    )(*args)


def begin(at, action):
    if at[1]:
        pl.when(pl.program_id(0) == 0)(action)


def finish(at, action):
    if at[2]:
        pl.when(pl.program_id(0) == pl.num_programs(0) - 1)(action)


def in_hbm(*arrays):
    return tuple(pltpu.with_memory_space_constraint(x, pltpu.HBM) for x in arrays)


def exchange(x, axis):
    return lax.all_to_all(x, axis, 0, 0, tiled=True)


def local(hidden, cotangent, norm_gain, mr_filter, residue, decay_rate, skip_weight):
    channels, tokens = hidden.shape
    groups, taps = mr_filter.shape
    modes = residue.shape[1]
    n_ctx = lax.axis_size("ctx")
    n_ch = lax.axis_size("ch")
    width = channels * n_ch
    scale = (tokens * n_ctx) ** (-0.5)
    nb = tokens // B
    steps = groups // GB
    shape = jax.ShapeDtypeStruct
    hidden, cotangent, mr_filter = in_hbm(hidden, cotangent, mr_filter)

    wide = (16 * GB, tokens)
    thin = (16 * GB, B)
    tall = (GB, 16 * (nb + 1), B)
    pair_tall = (GB // 2, 16 * (nb + 1), B)
    body = (GB, 16 * nb, B)
    quad = (GB // 4, 16, B)
    quad_two = (GB // 4, 32, B)
    quad_row = (GB // 4, 1, B)
    pay = (16, B)

    def full(*dims):
        return (None,) + dims

    tail, head, own_sq = call(
        prep_kernel,
        "prep",
        [wide, thin],
        (
            [thin, thin, full(nb, B)],
            [shape((channels, B), bf16), shape((channels, B), bf16), shape((nb, B), f32)],
        ),
        (hidden, cotangent),
        steps=steps,
        per=PER["prep"],
        moved=3 * 2**20,
        scratch=[pltpu.VMEM((8, tokens), f32)],
    )
    ct_next = lax.ppermute(head, "ctx", [(i, i - 1) for i in range(1, n_ctx)])
    h_prev = lax.ppermute(tail, "ctx", [(i, i + 1) for i in range(n_ctx - 1)])
    (edge,) = call(
        functools.partial(edge_kernel, nb),
        "edge",
        [full(channels, B), full(nb, B)],
        ([full(n_ch, 16, B)], [shape((n_ch, 16, B), f32)]),
        (h_prev, own_sq),
        moved=2**18,
    )
    edge, ct_next = lax.optimization_barrier((edge, ct_next))
    squares = exchange(edge, "ch")

    rate_flat = decay_rate.reshape(steps, B)
    res_flat = residue.reshape(steps, B)
    rate_four = jnp.tile(decay_rate, (1, 4)).reshape(groups // 2, B)
    rate_pair = jnp.concatenate([decay_rate, decay_rate], axis=1).reshape(groups // 4, B)
    rate_rows = rate_pair.reshape(groups // 4, 1, B)
    gain_flat = norm_gain.reshape(steps, B)
    skip_flat = skip_weight.reshape(steps, B)
    flat = full(steps, B)

    grad_local, after_local, packed = call(
        functools.partial(grads_kernel, nb),
        "grads",
        [wide, thin, flat, flat, full(groups // 2, B), flat],
        (
            [tall, pair_tall, quad],
            [
                pltpu.HBM((groups, 16 * (nb + 1), B), f32),
                pltpu.HBM((groups // 2, 16 * (nb + 1), B), f32),
                shape((groups // 4, 16, B), f32),
            ],
        ),
        (cotangent, ct_next, rate_flat, res_flat, rate_four, skip_flat),
        flops=groups * 2 * 144 * 256 * 384,
        steps=steps,
        per=PER["grads"],
        moved=14 * 2**20,
    )

    def moments(offset, before, x_next):
        held = [pl.BlockSpec(memory_space=pl.ANY)] * len(before)
        return call(
            functools.partial(moments_kernel, nb, width),
            "moments",
            [
                wide, thin, full(n_ch, 16, B), flat, wide, full(groups, B), quad_row,
                full(groups // 2, B), pair_tall,
            ]
            + held,
            (
                [tall, pay, quad_two],
                [
                    pltpu.HBM((groups, 16 * (nb + 1), B), bf16),
                    shape((16 * steps, B), f32),
                    shape((groups // 4, 32, B), f32),
                ],
            ),
            (
                hidden, x_next, squares, gain_flat, cotangent, mr_filter, rate_rows, rate_four,
                after_local, *before,
            ),
            steps=steps // 2,
            per=PER["moments"],
            offset=offset,
            flops=groups * 128 * 256 * 384,
            moved=7 * 2**20,
            scratch=[pltpu.VMEM((groups, B), f32)],
            aliases={9 + i: i for i in range(len(before))},
        )

    grad_local, after_local = in_hbm(grad_local, after_local)
    arrived = exchange(packed.reshape(n_ctx, 8, B), "ctx")
    early = moments(0, (), h_prev)
    early = in_hbm(early[0]) + tuple(early[1:])
    arrived, early = lax.optimization_barrier((arrived, tuple(early)))
    (scanned,) = call(
        functools.partial(scan_kernel, n_ctx, tokens),
        "scan",
        [full(n_ctx, 8, B), full(groups // 4, B)],
        ([full(n_ctx, 8, B)], [shape((n_ctx, 8, B), f32)]),
        (arrived, rate_pair),
        moved=2**18,
    )
    scanned, edge_rows = lax.optimization_barrier((scanned, h_prev))
    after = exchange(scanned, "ctx").reshape(groups // 4, 16, B)
    units, part, ends = moments(steps // 2, early, edge_rows)
    (units,) = in_hbm(units)

    ig, row_part, mostly, grad_mixed = call(
        functools.partial(inputs_kernel, nb, width),
        "inputs",
        [
            tall, quad, flat, flat, quad_row, wide, full(n_ch, 16, B), flat, full(groups, B),
            pay, quad_two,
        ],
        (
            [body, full(n_ch, nb, B), pay, body],
            [
                pltpu.HBM((groups, 16 * nb, B), f32),
                shape((n_ch, nb, B), f32),
                shape((16 * steps, B), f32),
                pltpu.HBM((groups, 16 * nb, B), bf16),
            ],
        ),
        (
            grad_local, after, rate_flat, res_flat, rate_rows, hidden,
            squares, gain_flat, mr_filter, part, ends,
        ),
        flops=groups * 2 * 144 * 256 * 512,
        steps=steps,
        per=PER["inputs"],
        moved=14 * 2**20,
        scratch=[pltpu.VMEM((8 * nb, B), f32), pltpu.VMEM((groups, B), f32)],
    )

    ig, grad_mixed = in_hbm(ig, grad_mixed)
    raw = exchange(row_part, "ch")
    extra = groups // 4
    lines = groups + 2 * steps + 2 * extra
    (payload,) = call(
        functools.partial(taps_kernel, nb),
        "taps",
        [body, tall, pay],
        ([full(n_ctx, lines, B)], [shape((n_ctx, lines, B), bf16)]),
        (grad_mixed, units, mostly),
        flops=groups * 2 * 128 * 128 * 256,
        steps=steps,
        per=PER["taps"],
        moved=5 * 2**20,
        scratch=[pltpu.VMEM((lines - extra, B), f32)],
    )
    raw, payload = lax.optimization_barrier((raw, payload))
    landed = exchange(payload, "ctx")
    grad_hidden, grad_inv_rms = call(
        functools.partial(final_kernel, nb, width),
        "final",
        [body, wide, full(n_ch, 16, B), flat, full(n_ch, nb, B)],
        (
            [wide, full(nb, B)],
            [shape((channels, tokens), bf16), shape((nb, B), f32)],
        ),
        (ig, hidden, squares, gain_flat, raw),
        steps=steps,
        per=PER["final"],
        moved=8 * 2**20,
    )
    landed, grad_inv_rms = lax.optimization_barrier((landed, grad_inv_rms))
    grad_mr, grad_gain, grad_skip, both = call(
        functools.partial(outs_kernel, scale),
        "outs",
        [full(n_ctx, lines, B)],
        (
            [full(groups, taps), full(steps, B), full(steps, B), full(groups // 4, B)],
            [
                shape((groups, taps), f32),
                shape((steps, B), f32),
                shape((steps, B), f32),
                shape((groups // 4, B), f32),
            ],
        ),
        (landed,),
        moved=2**20,
    )
    both = both.reshape(groups, 2 * modes)
    first, second = both[:, :modes], both[:, modes:]
    root_rate = jnp.sqrt(2.0 * decay_rate)
    return (
        grad_hidden,
        grad_gain.reshape(channels),
        grad_mr,
        root_rate * first,
        residue * root_rate * (0.5 * first - decay_rate * second),
        grad_skip.reshape(channels),
        grad_inv_rms.reshape(tokens),
    )


def solution(mesh):
    return jax.shard_map(
        local,
        mesh=mesh,
        in_specs=(
            P("ch", "ctx"),
            P("ch", "ctx"),
            P("ch"),
            P("ch", None),
            P("ch", None),
            P("ch", None),
            P("ch"),
        ),
        out_specs=(
            P("ch", "ctx"),
            P("ch"),
            P("ch", None),
            P("ch", None),
            P("ch", None),
            P("ch"),
            P("ctx"),
        ),
        check_vma=False,
    )
```

```python
import functools

import jax
import jax.numpy as jnp
from jax import lax
from jax.experimental import pallas as pl
from jax.experimental.pallas import tpu as pltpu
from jax.sharding import PartitionSpec as P

eps_norm = 1e-06
B = 128
GB = 8
VMEM = 30 * 1024 * 1024
PER = {"prep": 4, "grads": 2, "moments": 1, "inputs": 4, "taps": 2, "final": 4}
f32 = jnp.float32
bf16 = jnp.bfloat16

NN = (((1,), (0,)), ((), ()))
NT = (((1,), (1,)), ((), ()))
TN = (((0,), (0,)), ((), ()))


def mm(a, b, dims):
    return lax.dot_general(a, b, dims, preferred_element_type=f32)


def split(x):
    hi = x.astype(bf16)
    lo = (x - hi.astype(f32)).astype(bf16)
    return hi, lo


def iotas(shape):
    return (
        lax.broadcasted_iota(jnp.int32, shape, 0),
        lax.broadcasted_iota(jnp.int32, shape, 1),
    )


def spread(row):
    return jnp.transpose(jnp.broadcast_to(row, (B, B)))


def fine(x):
    hi, mid = split(x)
    low = (x - hi.astype(f32) - mid.astype(f32)).astype(bf16)
    return jnp.concatenate([hi, mid, low], axis=1)


def lane_sums(x):
    return mm(jnp.ones((8, 3 * B), bf16), fine(x), NT)[:1]


def turned_sums(x):
    return jnp.sum(jnp.transpose(x), axis=0, keepdims=True)


def toeplitz(row):
    full = jnp.broadcast_to(row, (B, B))
    return pltpu.roll(full, 0, 1, stride=1, stride_axis=0)


def lag_sums(square):
    total = square[:8]
    for a in range(8, B, 8):
        total = total + pltpu.roll(square[a : a + 8], B - a, 1)
    row = lax.broadcasted_iota(jnp.int32, (8, B), 0)
    for bit in (1, 2, 4):
        total = jnp.where((row & bit) != 0, pltpu.roll(total, B - bit, 1), total)
    return jnp.sum(total, axis=0, keepdims=True)


def prep_kernel(at, h_ref, ct_ref, tail_ref, head_ref, sq_ref, acc_ref):
    tokens = h_ref.shape[1]

    def clear():
        acc_ref[...] = jnp.zeros_like(acc_ref)

    begin(at, clear)
    h = h_ref[...].astype(f32)
    acc_ref[...] += jnp.sum(jnp.square(h).reshape(h.shape[0] // 8, 8, tokens), axis=0)
    tail_ref[...] = h_ref[:, tokens - B :]
    head_ref[...] = ct_ref[...]

    def write():
        row = jnp.sum(acc_ref[...], axis=0, keepdims=True)
        for b in range(tokens // B):
            sq_ref[pl.ds(b, 1), :] = row[:, B * b : B * b + B]

    finish(at, write)


def edge_kernel(nb, h_ref, sq_ref, out_ref):
    h = h_ref[...].astype(f32)
    part = jnp.sum(jnp.square(h).reshape(h.shape[0] // 8, 8, B), axis=0)
    edge = jnp.sum(part, axis=0, keepdims=True)
    rows = jnp.concatenate([edge, sq_ref[...], jnp.zeros((7, B), f32)], axis=0)
    for i in range(out_ref.shape[0]):
        out_ref[i] = rows


def inverse_rows(sq_ref, width):
    total = sq_ref[0]
    for i in range(1, sq_ref.shape[0]):
        total = total + sq_ref[i]
    return lax.rsqrt(total / width + eps_norm)


def grads_kernel(
    nb, at, ct_ref, ctn_ref, rate_ref, res_ref, four_ref, skip_ref, gml_ref, aft_ref, pack_ref
):
    step = at[0]
    row, lane = iotas((B, B))
    upper = lane <= row
    back = ((B - lane) % B).astype(f32)
    below = row.astype(f32)
    slot = lane % 64
    first_half = lane < 64
    step_lane = lax.broadcasted_iota(jnp.int32, (16, B), 1)
    step_slot = step_lane % 64
    third = (step_slot >= 32) & (step_slot < 48)
    zeros = jnp.zeros((16, B), f32)
    none = jnp.zeros((16, B), bf16)
    rates = spread(rate_ref[pl.ds(step, 1), :])
    amps = spread(res_ref[pl.ds(step, 1), :]) * jnp.sqrt(2.0 * rates)
    reach = amps * jnp.exp(-rates * (float(B) - lane.astype(f32)))
    lags = amps * jnp.exp(-rates * back)
    skips = spread(skip_ref[pl.ds(step, 1), :])

    def near_part(g, fall):
        rows = pl.ds(16 * g, 16)
        sub = slice(16 * g, 16 * g + 16)
        blocks = [ct_ref[rows, pl.ds(B * b, B)] for b in range(nb)] + [ctn_ref[rows, :]]
        lhs = jnp.concatenate(blocks, axis=0)
        kernel_row = jnp.sum(lags[sub], axis=0, keepdims=True)
        toe = jnp.where(upper, toeplitz(kernel_row), 0.0)
        mine = jnp.where(first_half if g % 2 == 0 else ~first_half, fall, 0.0)
        hi, lo = split(jnp.concatenate([toe, mine], axis=1))
        out = mm(jnp.concatenate([lhs, lhs], axis=1), jnp.concatenate([hi, lo], axis=0), NN)
        direct = jnp.concatenate([skips[sub]] * (nb + 1), axis=0) * lhs.astype(f32)
        gml_ref[g] = out[:, :B] + direct
        return out[:, B:]

    def first_stage(p):
        pair_rates = four_ref[pl.ds(4 * step + p, 1), :]
        fall = jnp.exp(-pair_rates * below)
        fall = jnp.where((slot >= 16) & (slot < 32), fall * below, fall)
        return near_part(2 * p, fall) + near_part(2 * p + 1, fall), pair_rates

    def second_stage(p, states, pair_rates):
        decay = jnp.broadcast_to(jnp.exp(-pair_rates * float(B)), (16, B))
        after = zeros
        found = [after]
        for b in range(nb, 0, -1):
            state = states[16 * b : 16 * b + 16]
            state = jnp.where(third, state * float(B * b), state)
            after = state + decay * after
            found.append(after)
        after_all = jnp.concatenate(found[::-1], axis=0)
        aft_ref[p] = after_all
        one = after + pltpu.roll(after, B - 16, 1) - float(B) * pltpu.roll(after, 16, 1)
        tile = jnp.where(step_slot < 16, after, jnp.where(step_slot < 32, one, 0.0))
        tile = tile + pltpu.roll(tile, B - 32, 1)
        tile = jnp.where(step_lane < 64, tile, 0.0)
        a_hi, a_lo = split(after_all)
        halves = []
        for h in range(2):
            g = 2 * p + h
            g_hi, g_lo = split(reach[16 * g : 16 * g + 16])
            upper_rows = [g_hi, none, none, g_lo]
            lower_rows = [g_hi, none, none, none]
            gap = [none] * 4
            if h == 0:
                parts = upper_rows + gap + lower_rows + gap
            else:
                parts = gap + upper_rows + gap + lower_rows
            halves.append(jnp.concatenate(parts, axis=0))
        far = mm(
            jnp.concatenate([a_hi, a_lo], axis=1), jnp.concatenate(halves, axis=1), NN
        )
        gml_ref[2 * p] += far[:, :B]
        gml_ref[2 * p + 1] += far[:, B:]
        return tile

    held = first_stage(0)
    tiles = []
    for p in range(GB // 2):
        ahead = first_stage(p + 1) if p + 1 < GB // 2 else None
        tiles.append(second_stage(p, *held))
        held = ahead
    for k in range(GB // 4):
        pack_ref[k] = tiles[2 * k] + pltpu.roll(tiles[2 * k + 1], 64, 1)


def squeeze(tile):
    lane = lax.broadcasted_iota(jnp.int32, tile.shape, 1)
    tile = jnp.where(lane % 64 < 32, tile, 0.0)
    return jnp.where(lane < 64, tile + pltpu.roll(tile, B - 32, 1), 0.0)


def moments_kernel(
    nb, width, at, h_ref, hp_ref, sq_ref, gain_ref, ct_ref, w_ref, pair_ref, four_ref,
    aft_ref, *refs,
):
    x_ref, part_ref, end_ref, w_scratch = refs[-4:]
    step = at[0]

    def load():
        w_scratch[...] = w_ref[...].astype(f32)

    begin(at, load)

    row, lane = iotas((B, B))
    upper = lane >= row
    togo = float(B) - row.astype(f32)
    slot = lane % 64
    first_half = lane < 64
    step_slot = lax.broadcasted_iota(jnp.int32, (16, B), 1) % 64
    low = step_slot < 16
    half = step_slot < 32
    second = half & (step_slot >= 16)
    zeros = jnp.zeros((16, B), f32)
    inverse = inverse_rows(sq_ref, width)
    gains = spread(gain_ref[pl.ds(step, 1), :])

    def mix(g):
        rows = pl.ds(16 * g, 16)
        sub = slice(16 * g, 16 * g + 16)
        units = []
        for b in range(nb + 1):
            h = hp_ref[rows, :] if b == 0 else h_ref[rows, pl.ds(B * (b - 1), B)]
            units.append((h.astype(f32) * inverse[b : b + 1] * gains[sub]).astype(bf16))
        x_all = jnp.concatenate(units, axis=0)
        x_ref[g] = x_all
        lhs = jnp.concatenate([x_all[: 16 * nb], x_all[16:]], axis=1)
        taps = toeplitz(w_scratch[pl.ds(GB * step + g, 1), :])
        cur = jnp.where(upper, taps, 0.0).astype(bf16)
        prev = jnp.where(upper, 0.0, taps).astype(bf16)
        return mm(lhs, jnp.concatenate([prev, cur], axis=0), NN).astype(bf16)

    def first_stage(p):
        pair_rates = four_ref[pl.ds(4 * step + p, 1), :]
        rise = jnp.exp(-pair_rates * togo)
        rise = jnp.where(slot >= 48, rise * togo, rise)
        hi, lo = split(
            jnp.concatenate(
                [jnp.where(first_half, rise, 0.0), jnp.where(first_half, 0.0, rise)], axis=0
            )
        )
        mixes = [mix(2 * p), mix(2 * p + 1)]
        lifted = mm(
            jnp.concatenate(mixes, axis=1), jnp.concatenate([hi, lo], axis=1), NN
        )
        return mixes, lifted[:, :B] + lifted[:, B:], pair_rates

    skip_parts = []
    corrs = []

    def second_stage(p, mixes, lifted, pair_rates):
        for h in range(2):
            rows = pl.ds(16 * (2 * p + h), 16)
            mixed = mixes[h]
            ct = jnp.concatenate([ct_ref[rows, pl.ds(B * b, B)] for b in range(nb)], axis=0)
            pairs = mm(mixed, ct, TN)
            direct = ct.astype(f32) * mixed.astype(f32)
            total = direct[:16]
            for b in range(1, nb):
                total = total + direct[16 * b : 16 * b + 16]
            skip_parts.append(total)
            corrs.append(lag_sums(jnp.where(upper, pairs, 0.0)))
        after = aft_ref[p]
        decay = jnp.broadcast_to(jnp.exp(-pair_rates * float(B)), (16, B))
        plain = zeros
        scaled = zeros
        end = zeros
        for b in range(nb):
            lift = lifted[16 * b : 16 * b + 16]
            prod = lift * after[16 * b : 16 * b + 16]
            plain = plain + prod
            scaled = scaled + prod * float(B * (b + 1))
            end = decay * (end + jnp.where(second, lift * float(B * (nb - b)), lift))
        plain = plain[:8] + plain[8:]
        scaled = scaled[:8] + scaled[8:]
        after_one = (
            plain + pltpu.roll(plain, B - 16, 1) + pltpu.roll(plain, B - 32, 1)
            - pltpu.roll(scaled, 16, 1)
        )
        found = squeeze(jnp.where(low[:8], plain, after_one))
        ends_zero = squeeze(jnp.where(low, end, pltpu.roll(end, B - 16, 1)))
        ends_one = squeeze(
            jnp.where(low, pltpu.roll(end, B - 16, 1) + pltpu.roll(end, B - 48, 1), 0.0)
        )
        return found, ends_zero, ends_one

    held = first_stage(0)
    tiles = []
    for p in range(GB // 2):
        nxt = first_stage(p + 1) if p + 1 < GB // 2 else None
        tiles.append(second_stage(p, *held))
        held = nxt
    quads = []
    for k in range(GB // 4):
        left, right = tiles[2 * k], tiles[2 * k + 1]
        joined = [a + pltpu.roll(b, 64, 1) for a, b in zip(left, right)]
        quads.append(jnp.sum(joined[0], axis=0, keepdims=True))
        end_ref[k] = jnp.concatenate(joined[1:], axis=0)
    skip_row = lane_sums(jnp.concatenate(skip_parts, axis=0))
    below = row.astype(f32)
    tables = []
    for k in range(GB // 4):
        fall = jnp.exp(-jnp.broadcast_to(pair_ref[k], (B, B)) * below)
        tables.append(jnp.where(lane % 32 < 16, fall, fall * below))
    t_hi, t_lo = split(jnp.concatenate(tables, axis=1))
    c_hi, c_lo = split(jnp.concatenate(corrs, axis=0))
    near = mm(
        jnp.concatenate([c_hi, c_lo, c_hi], axis=1),
        jnp.concatenate([t_hi, t_hi, t_lo], axis=0),
        NN,
    )
    n_row, n_lane = iotas((GB, 32 * GB))
    near = jnp.sum(jnp.where(n_lane // 32 == n_row, near, 0.0), axis=0, keepdims=True)
    blank = jnp.zeros((1, B), f32)
    part_ref[...] = jnp.concatenate(
        [blank] * 6 + [skip_row] + [blank] * 3 + [quads[0] + near[:, :B]]
        + [blank] * 3 + [quads[1] + near[:, B:]] + [blank],
        axis=0,
    )


def mirror_matrix():
    row, lane = iotas((B, B))
    return jnp.where((row + lane) % B == 0, 1.0, 0.0).astype(bf16)


def inputs_kernel(
    nb, width, at, gml_ref, a_ref, rate_ref, res_ref, pair_ref, h_ref, sq_ref, gain_ref, w_ref,
    part_ref, end_ref, ig_ref, row_ref, pay_ref, grad_ref, acc_ref, w_scratch,
):
    step = at[0]

    def load():
        w_scratch[...] = mm(w_ref[...], mirror_matrix(), NN)
        acc_ref[...] = jnp.zeros_like(acc_ref)

    begin(at, load)

    row, lane = iotas((B, B))
    upper = lane <= row
    none = jnp.zeros((16, B), bf16)
    ones = (lax.broadcasted_iota(jnp.int32, (16, B), 1) % 32) >= 16
    inverse = inverse_rows(sq_ref, width)
    gains = spread(gain_ref[pl.ds(step, 1), :])
    rates = spread(rate_ref[pl.ds(step, 1), :])
    amps = spread(res_ref[pl.ds(step, 1), :]) * jnp.sqrt(2.0 * rates)
    reach = amps * jnp.exp(-rates * (float(B) - lane.astype(f32)))
    sums = [acc_ref[pl.ds(8 * b, 8), :] for b in range(nb)]
    gain_parts = []
    quads = []
    lhs_of = {}

    def cross(k):
        decay = jnp.exp(jnp.broadcast_to(pair_ref[k], (16, B)) * (-float(B)))
        after = a_ref[k]
        ends = end_ref[k]
        first = jnp.sum(ends[:16] * after, axis=0, keepdims=True)
        other = jnp.sum(ends[16:] * after, axis=0, keepdims=True)
        quads.append(first + pltpu.roll(jnp.broadcast_to(other, (8, B)), 16, 1)[:1])
        after = jnp.where(ones, pltpu.roll(after, 16, 1), after)
        found = [after]
        for b in range(nb):
            after = after * decay
            found.append(after)
        a_hi, a_lo = split(jnp.concatenate(found[::-1], axis=0))
        return jnp.concatenate([a_hi, a_lo], axis=1)

    def first_stage(p):
        k = p // 2
        if k not in lhs_of:
            lhs_of[k] = cross(k)
        halves = []
        for h in range(2):
            g = 2 * p + h
            q = g % 4
            g_hi, g_lo = split(reach[16 * g : 16 * g + 16])
            pad = [none] * (2 * q)
            end = [none] * (6 - 2 * q)
            halves.append(
                jnp.concatenate(pad + [g_hi, g_lo] + end + pad + [g_hi, none] + end, axis=0)
            )
        far = mm(lhs_of[k], jnp.concatenate(halves, axis=1), NN)
        grads = []
        for h in range(2):
            g = 2 * p + h
            grad = (gml_ref[g] + far[:, B * h : B * h + B]).astype(bf16)
            grad_ref[g] = grad[: 16 * nb]
            grads.append(grad)
        return grads

    def second_stage(p, grads):
        for h in range(2):
            g = 2 * p + h
            rows = pl.ds(16 * g, 16)
            sub = slice(16 * g, 16 * g + 16)
            grad = grads[h]
            taps = toeplitz(w_scratch[pl.ds(GB * step + g, 1), :])
            cur = jnp.where(upper, taps, 0.0).astype(bf16)
            prev = jnp.where(upper, 0.0, taps).astype(bf16)
            lhs = jnp.concatenate([grad[: 16 * nb], grad[16:]], axis=1)
            ig = mm(lhs, jnp.concatenate([cur, prev], axis=0), NN)
            ig_ref[g] = ig
            part = jnp.zeros((16, B), f32)
            for b in range(nb):
                prod = ig[16 * b : 16 * b + 16] * h_ref[rows, pl.ds(B * b, B)].astype(f32)
                part = part + prod * inverse[b + 1 : b + 2]
                prod = prod * gains[sub]
                sums[b] = sums[b] + (prod[:8] + prod[8:])
            gain_parts.append(part)

    held = first_stage(0)
    for p in range(GB // 2):
        nxt = first_stage(p + 1) if p + 1 < GB // 2 else None
        second_stage(p, held)
        held = nxt
    for b in range(nb):
        acc_ref[pl.ds(8 * b, 8), :] = sums[b]
    gain_row = turned_sums(jnp.concatenate(gain_parts, axis=0))
    blank = jnp.zeros((1, B), f32)
    pay_ref[...] = part_ref[...] + jnp.concatenate(
        [blank, blank, gain_row] + [blank] * 7 + [quads[0]] + [blank] * 3 + [quads[1], blank],
        axis=0,
    )

    def write():
        raw = jnp.concatenate(
            [jnp.sum(sums[b], axis=0, keepdims=True) for b in range(nb)], axis=0
        )
        for i in range(row_ref.shape[0]):
            row_ref[i] = raw

    finish(at, write)


def taps_kernel(nb, steps, at, grad_ref, x_ref, pay_ref, keep_ref, send_ref, rows_ref):
    step = at[0]
    row, lane = iotas((B, B))
    lower = row >= lane

    def product(g):
        x_all = x_ref[g]
        x_pair = jnp.concatenate([x_all[16:], x_all[: 16 * nb]], axis=1)
        return mm(grad_ref[g], x_pair, TN)

    rows = []
    held = product(0)
    for g in range(GB):
        nxt = product(g + 1) if g + 1 < GB else None
        rows.append(lag_sums(jnp.where(lower, held[:, :B], held[:, B:])))
        held = nxt
    mirror = jnp.concatenate([mirror_matrix()] * 3, axis=0)
    taps = mm(fine(jnp.concatenate(rows, axis=0)), mirror, NN)
    half = keep_ref.shape[0]
    span = steps // 2
    base = (step // span) * half
    step = step % span
    rows_ref[pl.ds(pl.multiple_of(base + GB * step, GB), GB), :] = taps
    first = base + GB * span
    for line, row in ((step, 2), (span + step, 6), (2 * span + 2 * step, 10)):
        rows_ref[pl.ds(first + line, 1), :] = pay_ref[pl.ds(row, 1), :]
    rows_ref[pl.ds(first + 2 * span + 2 * step + 1, 1), :] = pay_ref[pl.ds(14, 1), :]

    def write():
        side = lax.axis_index("ctx") % 2
        keep_ref[...] = rows_ref[pl.ds(pl.multiple_of(half * side, GB), half), :]
        send_ref[...] = rows_ref[pl.ds(pl.multiple_of(half * (1 - side), GB), half), :]

    finish(at, write)


def copies_kernel(fine_rows, keep_ref, got_ref, out_ref):
    rows = keep_ref[...] + got_ref[...]
    hi, lo = split(rows[rows.shape[0] - fine_rows :])
    rows = jnp.concatenate([rows.astype(bf16), lo], axis=0)
    for i in range(out_ref.shape[0]):
        out_ref[i] = rows


def final_kernel(nb, width, at, ig_ref, h_ref, sq_ref, gain_ref, raw_ref, out_ref, rms_ref):
    step = at[0]
    inverse = inverse_rows(sq_ref, width)
    gains = spread(gain_ref[pl.ds(step, 1), :])
    raw = raw_ref[0]
    for i in range(1, raw_ref.shape[0]):
        raw = raw + raw_ref[i]
    rms_ref[...] = raw * width ** (-0.5)
    inv = [inverse[b + 1 : b + 2] for b in range(nb)]
    pull = [raw[b : b + 1] * inv[b] * inv[b] * (1.0 / width) for b in range(nb)]
    for g in range(GB):
        rows = pl.ds(16 * g, 16)
        gain = gains[16 * g : 16 * g + 16]
        for b in range(nb):
            cols = pl.ds(B * b, B)
            h = h_ref[rows, cols].astype(f32)
            ig = ig_ref[g, pl.ds(16 * b, 16), :]
            out_ref[rows, cols] = (inv[b] * (ig * gain - h * pull[b])).astype(bf16)


def scan_kernel(count, span, s_ref, r_ref, out_ref):
    lane = lax.broadcasted_iota(jnp.int32, (8, B), 1)
    ones = (lane % 32) >= 16
    rates = r_ref[pl.ds(lax.axis_index("ctx") // 2, 1), :]
    decay = jnp.exp(jnp.broadcast_to(rates, (8, B)) * (-float(span)))
    x = jnp.zeros((8, B), f32)
    found = [None] * count
    found[count - 1] = x
    for i in range(count - 2, -1, -1):
        x = s_ref[i + 1] + decay * x
        found[i] = x
    v = jnp.zeros((8, B), f32)
    out_ref[count - 1] = v
    for i in range(count - 2, -1, -1):
        v = decay * (v + float(span) * pltpu.roll(found[i + 1], 16, 1))
        out_ref[i] = found[i] + jnp.where(ones, v, 0.0)


def outs_kernel(scale, in_ref, tap_ref, gain_ref, skip_ref, mom_ref):
    for side in range(2):
        total = in_ref[side].astype(f32)
        for i in range(side + 2, in_ref.shape[0], 2):
            total = total + in_ref[i].astype(f32)
        total = total * scale
        start = 0
        for ref in (tap_ref, gain_ref, skip_ref, mom_ref):
            size = ref.shape[0] // 2
            found = total[start : start + size]
            start += size
            if ref is mom_ref:
                found = found + total[start:]
            ref[pl.ds(side * size, size), :] = found


def call(
    kernel, name, ins, outs, args, steps=0, per=1, offset=0, flops=0, moved=0, scratch=(),
    aliases={},
):
    def spec(entry):
        if isinstance(entry, pl.BlockSpec):
            return entry
        lead, rest = entry[0], tuple(entry[1:])
        if lead is None:
            return pl.BlockSpec(rest, lambda *i: (0,) * len(rest))
        return pl.BlockSpec(
            (lead * per,) + rest, lambda i: (i + offset // per,) + (0,) * len(rest)
        )

    entries = list(ins) + list(outs[0]) + [(None,)] * len(scratch)

    def body(*refs):
        if not steps:
            kernel(*refs)
            return
        for sub in range(per):
            views = []
            for entry, ref in zip(entries, refs):
                if isinstance(entry, pl.BlockSpec) or entry[0] is None or per == 1:
                    views.append(ref)
                else:
                    views.append(ref.at[pl.ds(sub * entry[0], entry[0])])
            kernel((pl.program_id(0) * per + sub + offset, sub == 0, sub == per - 1), *views)

    return pl.pallas_call(
        body,
        name=name,
        grid=(steps // per,) if steps else (),
        in_specs=[spec(entry) for entry in ins],
        out_specs=[spec(entry) for entry in outs[0]],
        out_shape=list(outs[1]),
        scratch_shapes=scratch,
        input_output_aliases=aliases,
        compiler_params=pltpu.CompilerParams(vmem_limit_bytes=VMEM),
        cost_estimate=pl.CostEstimate(flops=flops, bytes_accessed=moved, transcendentals=0),
    )(*args)


def begin(at, action):
    if at[1]:
        pl.when(pl.program_id(0) == 0)(action)


def finish(at, action):
    if at[2]:
        pl.when(pl.program_id(0) == pl.num_programs(0) - 1)(action)


def in_hbm(*arrays):
    return tuple(pltpu.with_memory_space_constraint(x, pltpu.HBM) for x in arrays)


def exchange(x, axis):
    return lax.all_to_all(x, axis, 0, 0, tiled=True)


def local(hidden, cotangent, norm_gain, mr_filter, residue, decay_rate, skip_weight):
    channels, tokens = hidden.shape
    groups, taps = mr_filter.shape
    modes = residue.shape[1]
    n_ctx = lax.axis_size("ctx")
    n_ch = lax.axis_size("ch")
    width = channels * n_ch
    scale = (tokens * n_ctx) ** (-0.5)
    nb = tokens // B
    steps = groups // GB
    shape = jax.ShapeDtypeStruct
    hidden, cotangent, mr_filter = in_hbm(hidden, cotangent, mr_filter)

    wide = (16 * GB, tokens)
    thin = (16 * GB, B)
    tall = (GB, 16 * (nb + 1), B)
    pair_tall = (GB // 2, 16 * (nb + 1), B)
    body = (GB, 16 * nb, B)
    quad = (GB // 4, 16, B)
    quad_two = (GB // 4, 32, B)
    quad_row = (GB // 4, 1, B)
    pay = (16, B)

    def full(*dims):
        return (None,) + dims

    tail, head, own_sq = call(
        prep_kernel,
        "prep",
        [wide, thin],
        (
            [thin, thin, full(nb, B)],
            [shape((channels, B), bf16), shape((channels, B), bf16), shape((nb, B), f32)],
        ),
        (hidden, cotangent),
        steps=steps,
        per=PER["prep"],
        moved=3 * 2**20,
        scratch=[pltpu.VMEM((8, tokens), f32)],
    )
    ct_next = lax.ppermute(head, "ctx", [(i, i - 1) for i in range(1, n_ctx)])
    h_prev = lax.ppermute(tail, "ctx", [(i, i + 1) for i in range(n_ctx - 1)])
    (edge,) = call(
        functools.partial(edge_kernel, nb),
        "edge",
        [full(channels, B), full(nb, B)],
        ([full(n_ch, 16, B)], [shape((n_ch, 16, B), f32)]),
        (h_prev, own_sq),
        moved=2**18,
    )
    edge, ct_next = lax.optimization_barrier((edge, ct_next))
    squares = exchange(edge, "ch")

    rate_flat = decay_rate.reshape(steps, B)
    res_flat = residue.reshape(steps, B)
    rate_four = jnp.tile(decay_rate, (1, 4)).reshape(groups // 2, B)
    rate_pair = jnp.concatenate([decay_rate, decay_rate], axis=1).reshape(groups // 4, B)
    rate_rows = rate_pair.reshape(groups // 4, 1, B)
    gain_flat = norm_gain.reshape(steps, B)
    skip_flat = skip_weight.reshape(steps, B)
    flat = full(steps, B)

    grad_local, after_local, packed = call(
        functools.partial(grads_kernel, nb),
        "grads",
        [wide, thin, flat, flat, full(groups // 2, B), flat],
        (
            [tall, pair_tall, quad],
            [
                pltpu.HBM((groups, 16 * (nb + 1), B), f32),
                pltpu.HBM((groups // 2, 16 * (nb + 1), B), f32),
                shape((groups // 4, 16, B), f32),
            ],
        ),
        (cotangent, ct_next, rate_flat, res_flat, rate_four, skip_flat),
        flops=groups * 2 * 144 * 256 * 384,
        steps=steps,
        per=PER["grads"],
        moved=14 * 2**20,
    )

    def moments(offset, before, x_next):
        held = [pl.BlockSpec(memory_space=pl.ANY)] * len(before)
        return call(
            functools.partial(moments_kernel, nb, width),
            "moments",
            [
                wide, thin, full(n_ch, 16, B), flat, wide, full(groups, B), quad_row,
                full(groups // 2, B), pair_tall,
            ]
            + held,
            (
                [tall, pay, quad_two],
                [
                    pltpu.HBM((groups, 16 * (nb + 1), B), bf16),
                    shape((16 * steps, B), f32),
                    shape((groups // 4, 32, B), f32),
                ],
            ),
            (
                hidden, x_next, squares, gain_flat, cotangent, mr_filter, rate_rows, rate_four,
                after_local, *before,
            ),
            steps=steps // 2,
            per=PER["moments"],
            offset=offset,
            flops=groups * 128 * 256 * 384,
            moved=7 * 2**20,
            scratch=[pltpu.VMEM((groups, B), f32)],
            aliases={9 + i: i for i in range(len(before))},
        )

    grad_local, after_local = in_hbm(grad_local, after_local)
    arrived = exchange(packed.reshape(n_ctx, 8, B), "ctx")
    early = moments(0, (), h_prev)
    early = in_hbm(early[0]) + tuple(early[1:])
    arrived, early = lax.optimization_barrier((arrived, tuple(early)))
    (scanned,) = call(
        functools.partial(scan_kernel, n_ctx, tokens),
        "scan",
        [full(n_ctx, 8, B), full(groups // 4, B)],
        ([full(n_ctx, 8, B)], [shape((n_ctx, 8, B), f32)]),
        (arrived, rate_pair),
        moved=2**18,
    )
    scanned, edge_rows = lax.optimization_barrier((scanned, h_prev))
    after = exchange(scanned, "ctx").reshape(groups // 4, 16, B)
    units, part, ends = moments(steps // 2, early, edge_rows)
    (units,) = in_hbm(units)

    ig, row_part, mostly, grad_mixed = call(
        functools.partial(inputs_kernel, nb, width),
        "inputs",
        [
            tall, quad, flat, flat, quad_row, wide, full(n_ch, 16, B), flat, full(groups, B),
            pay, quad_two,
        ],
        (
            [body, full(n_ch, nb, B), pay, body],
            [
                pltpu.HBM((groups, 16 * nb, B), f32),
                shape((n_ch, nb, B), f32),
                shape((16 * steps, B), f32),
                pltpu.HBM((groups, 16 * nb, B), bf16),
            ],
        ),
        (
            grad_local, after, rate_flat, res_flat, rate_rows, hidden,
            squares, gain_flat, mr_filter, part, ends,
        ),
        flops=groups * 2 * 144 * 256 * 512,
        steps=steps,
        per=PER["inputs"],
        moved=14 * 2**20,
        scratch=[pltpu.VMEM((8 * nb, B), f32), pltpu.VMEM((groups, B), f32)],
    )

    ig, grad_mixed = in_hbm(ig, grad_mixed)
    raw = exchange(row_part, "ch")
    extra = groups // 8
    half = groups // 2 + steps + extra
    lines = half + extra
    keep, send = call(
        functools.partial(taps_kernel, nb, steps),
        "taps",
        [body, tall, pay],
        ([full(half, B), full(half, B)], [shape((half, B), f32), shape((half, B), f32)]),
        (grad_mixed, units, mostly),
        flops=groups * 2 * 128 * 128 * 256,
        steps=steps,
        per=PER["taps"],
        moved=5 * 2**20,
        scratch=[pltpu.VMEM((2 * half, B), f32)],
    )
    got = lax.ppermute(send, "ctx", [(i, i ^ 1) for i in range(n_ctx)])
    (payload,) = call(
        functools.partial(copies_kernel, extra),
        "copies",
        [full(half, B), full(half, B)],
        ([full(n_ctx, lines, B)], [shape((n_ctx, lines, B), bf16)]),
        (keep, got),
        moved=2**19,
    )
    raw, payload, gain_late = lax.optimization_barrier((raw, payload, gain_flat))
    landed = exchange(payload, "ctx")
    grad_hidden, grad_inv_rms = call(
        functools.partial(final_kernel, nb, width),
        "final",
        [body, wide, full(n_ch, 16, B), flat, full(n_ch, nb, B)],
        (
            [wide, full(nb, B)],
            [shape((channels, tokens), bf16), shape((nb, B), f32)],
        ),
        (ig, hidden, squares, gain_late, raw),
        steps=steps,
        per=PER["final"],
        moved=8 * 2**20,
    )
    landed, grad_inv_rms = lax.optimization_barrier((landed, grad_inv_rms))
    grad_mr, grad_gain, grad_skip, both = call(
        functools.partial(outs_kernel, scale),
        "outs",
        [full(n_ctx, lines, B)],
        (
            [full(groups, taps), full(steps, B), full(steps, B), full(groups // 4, B)],
            [
                shape((groups, taps), f32),
                shape((steps, B), f32),
                shape((steps, B), f32),
                shape((groups // 4, B), f32),
            ],
        ),
        (landed,),
        moved=2**20,
    )
    both = both.reshape(groups, 2 * modes)
    first, second = both[:, :modes], both[:, modes:]
    root_rate = jnp.sqrt(2.0 * decay_rate)
    return (
        grad_hidden,
        grad_gain.reshape(channels),
        grad_mr,
        root_rate * first,
        residue * root_rate * (0.5 * first - decay_rate * second),
        grad_skip.reshape(channels),
        grad_inv_rms.reshape(tokens),
    )


def solution(mesh):
    return jax.shard_map(
        local,
        mesh=mesh,
        in_specs=(
            P("ch", "ctx"),
            P("ch", "ctx"),
            P("ch"),
            P("ch", None),
            P("ch", None),
            P("ch", None),
            P("ch"),
        ),
        out_specs=(
            P("ch", "ctx"),
            P("ch"),
            P("ch", None),
            P("ch", None),
            P("ch", None),
            P("ch"),
            P("ctx"),
        ),
        check_vma=False,
    )
```

```python
import functools

import jax
import jax.numpy as jnp
from jax import lax
from jax.experimental import pallas as pl
from jax.experimental.pallas import tpu as pltpu
from jax.sharding import PartitionSpec as P

eps_norm = 1e-06
B = 128
GB = 8
VMEM = 30 * 1024 * 1024
PER = {"prep": 4, "grads": 2, "moments": 1, "inputs": 4, "taps": 2, "final": 4}
f32 = jnp.float32
bf16 = jnp.bfloat16

NN = (((1,), (0,)), ((), ()))
NT = (((1,), (1,)), ((), ()))
TN = (((0,), (0,)), ((), ()))


def mm(a, b, dims):
    return lax.dot_general(a, b, dims, preferred_element_type=f32)


def split(x):
    hi = x.astype(bf16)
    lo = (x - hi.astype(f32)).astype(bf16)
    return hi, lo


def iotas(shape):
    return (
        lax.broadcasted_iota(jnp.int32, shape, 0),
        lax.broadcasted_iota(jnp.int32, shape, 1),
    )


def spread(row):
    return jnp.transpose(jnp.broadcast_to(row, (B, B)))


def fine(x):
    hi, mid = split(x)
    low = (x - hi.astype(f32) - mid.astype(f32)).astype(bf16)
    return jnp.concatenate([hi, mid, low], axis=1)


def lane_sums(x):
    return mm(jnp.ones((8, 3 * B), bf16), fine(x), NT)[:1]


def turned_sums(x):
    return jnp.sum(jnp.transpose(x), axis=0, keepdims=True)


def toeplitz(row):
    full = jnp.broadcast_to(row, (B, B))
    return pltpu.roll(full, 0, 1, stride=1, stride_axis=0)


def lag_sums(square):
    total = square[:8]
    for a in range(8, B, 8):
        total = total + pltpu.roll(square[a : a + 8], B - a, 1)
    row = lax.broadcasted_iota(jnp.int32, (8, B), 0)
    for bit in (1, 2, 4):
        total = jnp.where((row & bit) != 0, pltpu.roll(total, B - bit, 1), total)
    return jnp.sum(total, axis=0, keepdims=True)


def prep_kernel(at, h_ref, ct_ref, tail_ref, head_ref, sq_ref, acc_ref):
    tokens = h_ref.shape[1]

    def clear():
        acc_ref[...] = jnp.zeros_like(acc_ref)

    begin(at, clear)
    h = h_ref[...].astype(f32)
    acc_ref[...] += jnp.sum(jnp.square(h).reshape(h.shape[0] // 8, 8, tokens), axis=0)
    tail_ref[...] = h_ref[:, tokens - B :]
    head_ref[...] = ct_ref[...]

    def write():
        row = jnp.sum(acc_ref[...], axis=0, keepdims=True)
        for b in range(tokens // B):
            sq_ref[pl.ds(b, 1), :] = row[:, B * b : B * b + B]

    finish(at, write)


def edge_kernel(nb, h_ref, sq_ref, out_ref):
    h = h_ref[...].astype(f32)
    part = jnp.sum(jnp.square(h).reshape(h.shape[0] // 8, 8, B), axis=0)
    edge = jnp.sum(part, axis=0, keepdims=True)
    rows = jnp.concatenate([edge, sq_ref[...], jnp.zeros((7, B), f32)], axis=0)
    for i in range(out_ref.shape[0]):
        out_ref[i] = rows


def inverse_rows(sq_ref, width):
    total = sq_ref[0]
    for i in range(1, sq_ref.shape[0]):
        total = total + sq_ref[i]
    return lax.rsqrt(total / width + eps_norm)


def grads_kernel(
    nb, at, ct_ref, ctn_ref, rate_ref, res_ref, four_ref, skip_ref, gml_ref, aft_ref, pack_ref
):
    step = at[0]
    row, lane = iotas((B, B))
    upper = lane <= row
    back = ((B - lane) % B).astype(f32)
    below = row.astype(f32)
    slot = lane % 64
    first_half = lane < 64
    step_lane = lax.broadcasted_iota(jnp.int32, (16, B), 1)
    step_slot = step_lane % 64
    third = (step_slot >= 32) & (step_slot < 48)
    zeros = jnp.zeros((16, B), f32)
    none = jnp.zeros((16, B), bf16)
    rates = spread(rate_ref[pl.ds(step, 1), :])
    amps = spread(res_ref[pl.ds(step, 1), :]) * jnp.sqrt(2.0 * rates)
    reach = amps * jnp.exp(-rates * (float(B) - lane.astype(f32)))
    lags = amps * jnp.exp(-rates * back)
    skips = spread(skip_ref[pl.ds(step, 1), :])

    def near_part(g, fall):
        rows = pl.ds(16 * g, 16)
        sub = slice(16 * g, 16 * g + 16)
        blocks = [ct_ref[rows, pl.ds(B * b, B)] for b in range(nb)] + [ctn_ref[rows, :]]
        lhs = jnp.concatenate(blocks, axis=0)
        kernel_row = jnp.sum(lags[sub], axis=0, keepdims=True)
        toe = jnp.where(upper, toeplitz(kernel_row), 0.0)
        mine = jnp.where(first_half if g % 2 == 0 else ~first_half, fall, 0.0)
        hi, lo = split(jnp.concatenate([toe, mine], axis=1))
        out = mm(jnp.concatenate([lhs, lhs], axis=1), jnp.concatenate([hi, lo], axis=0), NN)
        direct = jnp.concatenate([skips[sub]] * (nb + 1), axis=0) * lhs.astype(f32)
        gml_ref[g] = out[:, :B] + direct
        return out[:, B:]

    def first_stage(p):
        pair_rates = four_ref[pl.ds(4 * step + p, 1), :]
        fall = jnp.exp(-pair_rates * below)
        fall = jnp.where((slot >= 16) & (slot < 32), fall * below, fall)
        return near_part(2 * p, fall) + near_part(2 * p + 1, fall), pair_rates

    def second_stage(p, states, pair_rates):
        decay = jnp.broadcast_to(jnp.exp(-pair_rates * float(B)), (16, B))
        after = zeros
        found = [after]
        for b in range(nb, 0, -1):
            state = states[16 * b : 16 * b + 16]
            state = jnp.where(third, state * float(B * b), state)
            after = state + decay * after
            found.append(after)
        after_all = jnp.concatenate(found[::-1], axis=0)
        aft_ref[p] = after_all
        one = after + pltpu.roll(after, B - 16, 1) - float(B) * pltpu.roll(after, 16, 1)
        tile = jnp.where(step_slot < 16, after, jnp.where(step_slot < 32, one, 0.0))
        tile = tile + pltpu.roll(tile, B - 32, 1)
        tile = jnp.where(step_lane < 64, tile, 0.0)
        a_hi, a_lo = split(after_all)
        halves = []
        for h in range(2):
            g = 2 * p + h
            g_hi, g_lo = split(reach[16 * g : 16 * g + 16])
            upper_rows = [g_hi, none, none, g_lo]
            lower_rows = [g_hi, none, none, none]
            gap = [none] * 4
            if h == 0:
                parts = upper_rows + gap + lower_rows + gap
            else:
                parts = gap + upper_rows + gap + lower_rows
            halves.append(jnp.concatenate(parts, axis=0))
        far = mm(
            jnp.concatenate([a_hi, a_lo], axis=1), jnp.concatenate(halves, axis=1), NN
        )
        gml_ref[2 * p] += far[:, :B]
        gml_ref[2 * p + 1] += far[:, B:]
        return tile

    held = first_stage(0)
    tiles = []
    for p in range(GB // 2):
        ahead = first_stage(p + 1) if p + 1 < GB // 2 else None
        tiles.append(second_stage(p, *held))
        held = ahead
    for k in range(GB // 4):
        pack_ref[k] = tiles[2 * k] + pltpu.roll(tiles[2 * k + 1], 64, 1)


def squeeze(tile):
    lane = lax.broadcasted_iota(jnp.int32, tile.shape, 1)
    tile = jnp.where(lane % 64 < 32, tile, 0.0)
    return jnp.where(lane < 64, tile + pltpu.roll(tile, B - 32, 1), 0.0)


def moments_kernel(
    nb, width, at, h_ref, hp_ref, sq_ref, gain_ref, ct_ref, w_ref, pair_ref, four_ref,
    aft_ref, *refs,
):
    x_ref, part_ref, end_ref, w_scratch = refs[-4:]
    step = at[0]

    def load():
        w_scratch[...] = w_ref[...].astype(f32)

    begin(at, load)

    row, lane = iotas((B, B))
    upper = lane >= row
    togo = float(B) - row.astype(f32)
    slot = lane % 64
    first_half = lane < 64
    step_slot = lax.broadcasted_iota(jnp.int32, (16, B), 1) % 64
    low = step_slot < 16
    half = step_slot < 32
    second = half & (step_slot >= 16)
    zeros = jnp.zeros((16, B), f32)
    inverse = inverse_rows(sq_ref, width)
    gains = spread(gain_ref[pl.ds(step, 1), :])

    def mix(g):
        rows = pl.ds(16 * g, 16)
        sub = slice(16 * g, 16 * g + 16)
        units = []
        for b in range(nb + 1):
            h = hp_ref[rows, :] if b == 0 else h_ref[rows, pl.ds(B * (b - 1), B)]
            units.append((h.astype(f32) * inverse[b : b + 1] * gains[sub]).astype(bf16))
        x_all = jnp.concatenate(units, axis=0)
        x_ref[g] = x_all
        lhs = jnp.concatenate([x_all[: 16 * nb], x_all[16:]], axis=1)
        taps = toeplitz(w_scratch[pl.ds(GB * step + g, 1), :])
        cur = jnp.where(upper, taps, 0.0).astype(bf16)
        prev = jnp.where(upper, 0.0, taps).astype(bf16)
        return mm(lhs, jnp.concatenate([prev, cur], axis=0), NN).astype(bf16)

    def first_stage(p):
        pair_rates = four_ref[pl.ds(4 * step + p, 1), :]
        rise = jnp.exp(-pair_rates * togo)
        rise = jnp.where(slot >= 48, rise * togo, rise)
        hi, lo = split(
            jnp.concatenate(
                [jnp.where(first_half, rise, 0.0), jnp.where(first_half, 0.0, rise)], axis=0
            )
        )
        mixes = [mix(2 * p), mix(2 * p + 1)]
        return mixes, jnp.concatenate([hi, lo], axis=1), pair_rates

    skip_parts = []
    corrs = []

    def second_stage(p, mixes, weights, pair_rates):
        lifted = mm(jnp.concatenate(mixes, axis=1), weights, NN)
        lifted = lifted[:, :B] + lifted[:, B:]
        for h in range(2):
            rows = pl.ds(16 * (2 * p + h), 16)
            mixed = mixes[h]
            ct = jnp.concatenate([ct_ref[rows, pl.ds(B * b, B)] for b in range(nb)], axis=0)
            pairs = mm(mixed, ct, TN)
            direct = ct.astype(f32) * mixed.astype(f32)
            total = direct[:16]
            for b in range(1, nb):
                total = total + direct[16 * b : 16 * b + 16]
            skip_parts.append(total)
            corrs.append(lag_sums(jnp.where(upper, pairs, 0.0)))
        after = aft_ref[p]
        decay = jnp.broadcast_to(jnp.exp(-pair_rates * float(B)), (16, B))
        plain = zeros
        scaled = zeros
        end = zeros
        for b in range(nb):
            lift = lifted[16 * b : 16 * b + 16]
            prod = lift * after[16 * b : 16 * b + 16]
            plain = plain + prod
            scaled = scaled + prod * float(B * (b + 1))
            end = decay * (end + jnp.where(second, lift * float(B * (nb - b)), lift))
        plain = plain[:8] + plain[8:]
        scaled = scaled[:8] + scaled[8:]
        after_one = (
            plain + pltpu.roll(plain, B - 16, 1) + pltpu.roll(plain, B - 32, 1)
            - pltpu.roll(scaled, 16, 1)
        )
        found = squeeze(jnp.where(low[:8], plain, after_one))
        ends_zero = squeeze(jnp.where(low, end, pltpu.roll(end, B - 16, 1)))
        ends_one = squeeze(
            jnp.where(low, pltpu.roll(end, B - 16, 1) + pltpu.roll(end, B - 48, 1), 0.0)
        )
        return found, ends_zero, ends_one

    held = first_stage(0)
    tiles = []
    for p in range(GB // 2):
        nxt = first_stage(p + 1) if p + 1 < GB // 2 else None
        tiles.append(second_stage(p, *held))
        held = nxt
    quads = []
    for k in range(GB // 4):
        left, right = tiles[2 * k], tiles[2 * k + 1]
        joined = [a + pltpu.roll(b, 64, 1) for a, b in zip(left, right)]
        quads.append(jnp.sum(joined[0], axis=0, keepdims=True))
        end_ref[k] = jnp.concatenate(joined[1:], axis=0)
    skip_row = lane_sums(jnp.concatenate(skip_parts, axis=0))
    below = row.astype(f32)
    tables = []
    for k in range(GB // 4):
        fall = jnp.exp(-jnp.broadcast_to(pair_ref[k], (B, B)) * below)
        tables.append(jnp.where(lane % 32 < 16, fall, fall * below))
    t_hi, t_lo = split(jnp.concatenate(tables, axis=1))
    c_hi, c_lo = split(jnp.concatenate(corrs, axis=0))
    near = mm(
        jnp.concatenate([c_hi, c_lo, c_hi], axis=1),
        jnp.concatenate([t_hi, t_hi, t_lo], axis=0),
        NN,
    )
    n_row, n_lane = iotas((GB, 32 * GB))
    near = jnp.sum(jnp.where(n_lane // 32 == n_row, near, 0.0), axis=0, keepdims=True)
    blank = jnp.zeros((1, B), f32)
    part_ref[...] = jnp.concatenate(
        [blank] * 6 + [skip_row] + [blank] * 3 + [quads[0] + near[:, :B]]
        + [blank] * 3 + [quads[1] + near[:, B:]] + [blank],
        axis=0,
    )


def mirror_matrix():
    row, lane = iotas((B, B))
    return jnp.where((row + lane) % B == 0, 1.0, 0.0).astype(bf16)


def inputs_kernel(
    nb, width, at, gml_ref, a_ref, rate_ref, res_ref, pair_ref, h_ref, sq_ref, gain_ref, w_ref,
    part_ref, end_ref, ig_ref, row_ref, pay_ref, grad_ref, acc_ref, w_scratch,
):
    step = at[0]

    def load():
        w_scratch[...] = mm(w_ref[...], mirror_matrix(), NN)
        acc_ref[...] = jnp.zeros_like(acc_ref)

    begin(at, load)

    row, lane = iotas((B, B))
    upper = lane <= row
    none = jnp.zeros((16, B), bf16)
    ones = (lax.broadcasted_iota(jnp.int32, (16, B), 1) % 32) >= 16
    inverse = inverse_rows(sq_ref, width)
    gains = spread(gain_ref[pl.ds(step, 1), :])
    rates = spread(rate_ref[pl.ds(step, 1), :])
    amps = spread(res_ref[pl.ds(step, 1), :]) * jnp.sqrt(2.0 * rates)
    reach = amps * jnp.exp(-rates * (float(B) - lane.astype(f32)))
    sums = [acc_ref[pl.ds(8 * b, 8), :] for b in range(nb)]
    gain_parts = []
    quads = []
    lhs_of = {}

    def cross(k):
        decay = jnp.exp(jnp.broadcast_to(pair_ref[k], (16, B)) * (-float(B)))
        after = a_ref[k]
        ends = end_ref[k]
        first = jnp.sum(ends[:16] * after, axis=0, keepdims=True)
        other = jnp.sum(ends[16:] * after, axis=0, keepdims=True)
        quads.append(first + pltpu.roll(jnp.broadcast_to(other, (8, B)), 16, 1)[:1])
        after = jnp.where(ones, pltpu.roll(after, 16, 1), after)
        found = [after]
        for b in range(nb):
            after = after * decay
            found.append(after)
        a_hi, a_lo = split(jnp.concatenate(found[::-1], axis=0))
        return jnp.concatenate([a_hi, a_lo], axis=1)

    def first_stage(p):
        k = p // 2
        if k not in lhs_of:
            lhs_of[k] = cross(k)
        halves = []
        for h in range(2):
            g = 2 * p + h
            q = g % 4
            g_hi, g_lo = split(reach[16 * g : 16 * g + 16])
            pad = [none] * (2 * q)
            end = [none] * (6 - 2 * q)
            halves.append(
                jnp.concatenate(pad + [g_hi, g_lo] + end + pad + [g_hi, none] + end, axis=0)
            )
        far = mm(lhs_of[k], jnp.concatenate(halves, axis=1), NN)
        grads = []
        for h in range(2):
            g = 2 * p + h
            grad = (gml_ref[g] + far[:, B * h : B * h + B]).astype(bf16)
            grad_ref[g] = grad[: 16 * nb]
            grads.append(grad)
        return grads

    def second_stage(p, grads):
        for h in range(2):
            g = 2 * p + h
            rows = pl.ds(16 * g, 16)
            sub = slice(16 * g, 16 * g + 16)
            grad = grads[h]
            taps = toeplitz(w_scratch[pl.ds(GB * step + g, 1), :])
            cur = jnp.where(upper, taps, 0.0).astype(bf16)
            prev = jnp.where(upper, 0.0, taps).astype(bf16)
            lhs = jnp.concatenate([grad[: 16 * nb], grad[16:]], axis=1)
            ig = mm(lhs, jnp.concatenate([cur, prev], axis=0), NN)
            ig_ref[g] = ig
            part = jnp.zeros((16, B), f32)
            for b in range(nb):
                prod = ig[16 * b : 16 * b + 16] * h_ref[rows, pl.ds(B * b, B)].astype(f32)
                part = part + prod * inverse[b + 1 : b + 2]
                prod = prod * gains[sub]
                sums[b] = sums[b] + (prod[:8] + prod[8:])
            gain_parts.append(part)

    held = first_stage(0)
    for p in range(GB // 2):
        nxt = first_stage(p + 1) if p + 1 < GB // 2 else None
        second_stage(p, held)
        held = nxt
    for b in range(nb):
        acc_ref[pl.ds(8 * b, 8), :] = sums[b]
    gain_row = turned_sums(jnp.concatenate(gain_parts, axis=0))
    blank = jnp.zeros((1, B), f32)
    pay_ref[...] = part_ref[...] + jnp.concatenate(
        [blank, blank, gain_row] + [blank] * 7 + [quads[0]] + [blank] * 3 + [quads[1], blank],
        axis=0,
    )

    def write():
        raw = jnp.concatenate(
            [jnp.sum(sums[b], axis=0, keepdims=True) for b in range(nb)], axis=0
        )
        for i in range(row_ref.shape[0]):
            row_ref[i] = raw

    finish(at, write)


def taps_kernel(nb, steps, at, grad_ref, x_ref, pay_ref, keep_ref, send_ref, rows_ref):
    step = at[0]
    row, lane = iotas((B, B))
    lower = row >= lane

    def product(g):
        x_all = x_ref[g]
        x_pair = jnp.concatenate([x_all[16:], x_all[: 16 * nb]], axis=1)
        return mm(grad_ref[g], x_pair, TN)

    rows = []
    held = product(0)
    for g in range(GB):
        nxt = product(g + 1) if g + 1 < GB else None
        rows.append(lag_sums(jnp.where(lower, held[:, :B], held[:, B:])))
        held = nxt
    mirror = jnp.concatenate([mirror_matrix()] * 3, axis=0)
    taps = mm(fine(jnp.concatenate(rows, axis=0)), mirror, NN)
    half = keep_ref.shape[0]
    span = steps // 2
    base = (step // span) * half
    step = step % span
    rows_ref[pl.ds(pl.multiple_of(base + GB * step, GB), GB), :] = taps
    first = base + GB * span
    for line, row in ((step, 2), (span + step, 6), (2 * span + 2 * step, 10)):
        rows_ref[pl.ds(first + line, 1), :] = pay_ref[pl.ds(row, 1), :]
    rows_ref[pl.ds(first + 2 * span + 2 * step + 1, 1), :] = pay_ref[pl.ds(14, 1), :]

    def write():
        side = lax.axis_index("ctx") % 2
        keep_ref[...] = rows_ref[pl.ds(pl.multiple_of(half * side, GB), half), :]
        send_ref[...] = rows_ref[pl.ds(pl.multiple_of(half * (1 - side), GB), half), :]

    finish(at, write)


def copies_kernel(fine_rows, keep_ref, got_ref, out_ref):
    rows = keep_ref[...] + got_ref[...]
    hi, lo = split(rows[rows.shape[0] - fine_rows :])
    rows = jnp.concatenate([rows.astype(bf16), lo], axis=0)
    for i in range(out_ref.shape[0]):
        out_ref[i] = rows


def final_kernel(nb, width, at, ig_ref, h_ref, sq_ref, gain_ref, raw_ref, out_ref, rms_ref):
    step = at[0]
    inverse = inverse_rows(sq_ref, width)
    gains = spread(gain_ref[pl.ds(step, 1), :])
    raw = raw_ref[0]
    for i in range(1, raw_ref.shape[0]):
        raw = raw + raw_ref[i]
    rms_ref[...] = raw * width ** (-0.5)
    inv = [inverse[b + 1 : b + 2] for b in range(nb)]
    pull = [raw[b : b + 1] * inv[b] * inv[b] * (1.0 / width) for b in range(nb)]
    for g in range(GB):
        rows = pl.ds(16 * g, 16)
        gain = gains[16 * g : 16 * g + 16]
        for b in range(nb):
            cols = pl.ds(B * b, B)
            h = h_ref[rows, cols].astype(f32)
            ig = ig_ref[g, pl.ds(16 * b, 16), :]
            out_ref[rows, cols] = (inv[b] * (ig * gain - h * pull[b])).astype(bf16)


def scan_kernel(count, span, s_ref, r_ref, out_ref):
    lane = lax.broadcasted_iota(jnp.int32, (8, B), 1)
    ones = (lane % 32) >= 16
    rates = r_ref[pl.ds(lax.axis_index("ctx") // 2, 1), :]
    decay = jnp.exp(jnp.broadcast_to(rates, (8, B)) * (-float(span)))
    x = jnp.zeros((8, B), f32)
    found = [None] * count
    found[count - 1] = x
    for i in range(count - 2, -1, -1):
        x = s_ref[i + 1] + decay * x
        found[i] = x
    v = jnp.zeros((8, B), f32)
    out_ref[count - 1] = v
    for i in range(count - 2, -1, -1):
        v = decay * (v + float(span) * pltpu.roll(found[i + 1], 16, 1))
        out_ref[i] = found[i] + jnp.where(ones, v, 0.0)


def outs_kernel(scale, in_ref, tap_ref, gain_ref, skip_ref, mom_ref):
    for side in range(2):
        total = in_ref[side].astype(f32)
        for i in range(side + 2, in_ref.shape[0], 2):
            total = total + in_ref[i].astype(f32)
        total = total * scale
        start = 0
        for ref in (tap_ref, gain_ref, skip_ref, mom_ref):
            size = ref.shape[0] // 2
            found = total[start : start + size]
            start += size
            if ref is mom_ref:
                found = found + total[start:]
            ref[pl.ds(side * size, size), :] = found


def call(
    kernel, name, ins, outs, args, steps=0, per=1, offset=0, flops=0, moved=0, scratch=(),
    aliases={},
):
    def spec(entry):
        if isinstance(entry, pl.BlockSpec):
            return entry
        lead, rest = entry[0], tuple(entry[1:])
        if lead is None:
            return pl.BlockSpec(rest, lambda *i: (0,) * len(rest))
        return pl.BlockSpec(
            (lead * per,) + rest, lambda i: (i + offset // per,) + (0,) * len(rest)
        )

    entries = list(ins) + list(outs[0]) + [(None,)] * len(scratch)

    def body(*refs):
        if not steps:
            kernel(*refs)
            return
        for sub in range(per):
            views = []
            for entry, ref in zip(entries, refs):
                if isinstance(entry, pl.BlockSpec) or entry[0] is None or per == 1:
                    views.append(ref)
                else:
                    views.append(ref.at[pl.ds(sub * entry[0], entry[0])])
            kernel((pl.program_id(0) * per + sub + offset, sub == 0, sub == per - 1), *views)

    return pl.pallas_call(
        body,
        name=name,
        grid=(steps // per,) if steps else (),
        in_specs=[spec(entry) for entry in ins],
        out_specs=[spec(entry) for entry in outs[0]],
        out_shape=list(outs[1]),
        scratch_shapes=scratch,
        input_output_aliases=aliases,
        compiler_params=pltpu.CompilerParams(vmem_limit_bytes=VMEM),
        cost_estimate=pl.CostEstimate(flops=flops, bytes_accessed=moved, transcendentals=0),
    )(*args)


def begin(at, action):
    if at[1]:
        pl.when(pl.program_id(0) == 0)(action)


def finish(at, action):
    if at[2]:
        pl.when(pl.program_id(0) == pl.num_programs(0) - 1)(action)


def in_hbm(*arrays):
    return tuple(pltpu.with_memory_space_constraint(x, pltpu.HBM) for x in arrays)


def exchange(x, axis):
    return lax.all_to_all(x, axis, 0, 0, tiled=True)


def local(hidden, cotangent, norm_gain, mr_filter, residue, decay_rate, skip_weight):
    channels, tokens = hidden.shape
    groups, taps = mr_filter.shape
    modes = residue.shape[1]
    n_ctx = lax.axis_size("ctx")
    n_ch = lax.axis_size("ch")
    width = channels * n_ch
    scale = (tokens * n_ctx) ** (-0.5)
    nb = tokens // B
    steps = groups // GB
    shape = jax.ShapeDtypeStruct
    hidden, cotangent, mr_filter = in_hbm(hidden, cotangent, mr_filter)

    wide = (16 * GB, tokens)
    thin = (16 * GB, B)
    tall = (GB, 16 * (nb + 1), B)
    pair_tall = (GB // 2, 16 * (nb + 1), B)
    body = (GB, 16 * nb, B)
    quad = (GB // 4, 16, B)
    quad_two = (GB // 4, 32, B)
    quad_row = (GB // 4, 1, B)
    pay = (16, B)

    def full(*dims):
        return (None,) + dims

    tail, head, own_sq = call(
        prep_kernel,
        "prep",
        [wide, thin],
        (
            [thin, thin, full(nb, B)],
            [shape((channels, B), bf16), shape((channels, B), bf16), shape((nb, B), f32)],
        ),
        (hidden, cotangent),
        steps=steps,
        per=PER["prep"],
        moved=3 * 2**20,
        scratch=[pltpu.VMEM((8, tokens), f32)],
    )
    ct_next = lax.ppermute(head, "ctx", [(i, i - 1) for i in range(1, n_ctx)])
    h_prev = lax.ppermute(tail, "ctx", [(i, i + 1) for i in range(n_ctx - 1)])
    (edge,) = call(
        functools.partial(edge_kernel, nb),
        "edge",
        [full(channels, B), full(nb, B)],
        ([full(n_ch, 16, B)], [shape((n_ch, 16, B), f32)]),
        (h_prev, own_sq),
        moved=2**18,
    )
    edge, ct_next = lax.optimization_barrier((edge, ct_next))
    squares = exchange(edge, "ch")

    rate_flat = decay_rate.reshape(steps, B)
    res_flat = residue.reshape(steps, B)
    rate_four = jnp.tile(decay_rate, (1, 4)).reshape(groups // 2, B)
    rate_pair = jnp.concatenate([decay_rate, decay_rate], axis=1).reshape(groups // 4, B)
    rate_rows = rate_pair.reshape(groups // 4, 1, B)
    gain_flat = norm_gain.reshape(steps, B)
    skip_flat = skip_weight.reshape(steps, B)
    flat = full(steps, B)

    grad_local, after_local, packed = call(
        functools.partial(grads_kernel, nb),
        "grads",
        [wide, thin, flat, flat, full(groups // 2, B), flat],
        (
            [tall, pair_tall, quad],
            [
                pltpu.HBM((groups, 16 * (nb + 1), B), f32),
                pltpu.HBM((groups // 2, 16 * (nb + 1), B), f32),
                shape((groups // 4, 16, B), f32),
            ],
        ),
        (cotangent, ct_next, rate_flat, res_flat, rate_four, skip_flat),
        flops=groups * 2 * 144 * 256 * 384,
        steps=steps,
        per=PER["grads"],
        moved=14 * 2**20,
    )

    def moments(offset, before, x_next):
        held = [pl.BlockSpec(memory_space=pl.ANY)] * len(before)
        return call(
            functools.partial(moments_kernel, nb, width),
            "moments",
            [
                wide, thin, full(n_ch, 16, B), flat, wide, full(groups, B), quad_row,
                full(groups // 2, B), pair_tall,
            ]
            + held,
            (
                [tall, pay, quad_two],
                [
                    pltpu.HBM((groups, 16 * (nb + 1), B), bf16),
                    shape((16 * steps, B), f32),
                    shape((groups // 4, 32, B), f32),
                ],
            ),
            (
                hidden, x_next, squares, gain_flat, cotangent, mr_filter, rate_rows, rate_four,
                after_local, *before,
            ),
            steps=steps // 2,
            per=PER["moments"],
            offset=offset,
            flops=groups * 128 * 256 * 384,
            moved=7 * 2**20,
            scratch=[pltpu.VMEM((groups, B), f32)],
            aliases={9 + i: i for i in range(len(before))},
        )

    grad_local, after_local = in_hbm(grad_local, after_local)
    arrived = exchange(packed.reshape(n_ctx, 8, B), "ctx")
    early = moments(0, (), h_prev)
    early = in_hbm(early[0]) + tuple(early[1:])
    arrived, early = lax.optimization_barrier((arrived, tuple(early)))
    (scanned,) = call(
        functools.partial(scan_kernel, n_ctx, tokens),
        "scan",
        [full(n_ctx, 8, B), full(groups // 4, B)],
        ([full(n_ctx, 8, B)], [shape((n_ctx, 8, B), f32)]),
        (arrived, rate_pair),
        moved=2**18,
    )
    scanned, edge_rows = lax.optimization_barrier((scanned, h_prev))
    after = exchange(scanned, "ctx").reshape(groups // 4, 16, B)
    units, part, ends = moments(steps // 2, early, edge_rows)
    (units,) = in_hbm(units)

    ig, row_part, mostly, grad_mixed = call(
        functools.partial(inputs_kernel, nb, width),
        "inputs",
        [
            tall, quad, flat, flat, quad_row, wide, full(n_ch, 16, B), flat, full(groups, B),
            pay, quad_two,
        ],
        (
            [body, full(n_ch, nb, B), pay, body],
            [
                pltpu.HBM((groups, 16 * nb, B), f32),
                shape((n_ch, nb, B), f32),
                shape((16 * steps, B), f32),
                pltpu.HBM((groups, 16 * nb, B), bf16),
            ],
        ),
        (
            grad_local, after, rate_flat, res_flat, rate_rows, hidden,
            squares, gain_flat, mr_filter, part, ends,
        ),
        flops=groups * 2 * 144 * 256 * 512,
        steps=steps,
        per=PER["inputs"],
        moved=14 * 2**20,
        scratch=[pltpu.VMEM((8 * nb, B), f32), pltpu.VMEM((groups, B), f32)],
    )

    ig, grad_mixed = in_hbm(ig, grad_mixed)
    raw = exchange(row_part, "ch")
    extra = groups // 8
    half = groups // 2 + steps + extra
    lines = half + extra
    keep, send = call(
        functools.partial(taps_kernel, nb, steps),
        "taps",
        [body, tall, pay],
        ([full(half, B), full(half, B)], [shape((half, B), f32), shape((half, B), f32)]),
        (grad_mixed, units, mostly),
        flops=groups * 2 * 128 * 128 * 256,
        steps=steps,
        per=PER["taps"],
        moved=5 * 2**20,
        scratch=[pltpu.VMEM((2 * half, B), f32)],
    )
    got = lax.ppermute(send, "ctx", [(i, i ^ 1) for i in range(n_ctx)])
    (payload,) = call(
        functools.partial(copies_kernel, extra),
        "copies",
        [full(half, B), full(half, B)],
        ([full(n_ctx, lines, B)], [shape((n_ctx, lines, B), bf16)]),
        (keep, got),
        moved=2**19,
    )
    raw, payload, gain_late = lax.optimization_barrier((raw, payload, gain_flat))
    landed = exchange(payload, "ctx")
    grad_hidden, grad_inv_rms = call(
        functools.partial(final_kernel, nb, width),
        "final",
        [body, wide, full(n_ch, 16, B), flat, full(n_ch, nb, B)],
        (
            [wide, full(nb, B)],
            [shape((channels, tokens), bf16), shape((nb, B), f32)],
        ),
        (ig, hidden, squares, gain_late, raw),
        steps=steps,
        per=PER["final"],
        moved=8 * 2**20,
    )
    landed, grad_inv_rms = lax.optimization_barrier((landed, grad_inv_rms))
    grad_mr, grad_gain, grad_skip, both = call(
        functools.partial(outs_kernel, scale),
        "outs",
        [full(n_ctx, lines, B)],
        (
            [full(groups, taps), full(steps, B), full(steps, B), full(groups // 4, B)],
            [
                shape((groups, taps), f32),
                shape((steps, B), f32),
                shape((steps, B), f32),
                shape((groups // 4, B), f32),
            ],
        ),
        (landed,),
        moved=2**20,
    )
    both = both.reshape(groups, 2 * modes)
    first, second = both[:, :modes], both[:, modes:]
    root_rate = jnp.sqrt(2.0 * decay_rate)
    return (
        grad_hidden,
        grad_gain.reshape(channels),
        grad_mr,
        root_rate * first,
        residue * root_rate * (0.5 * first - decay_rate * second),
        grad_skip.reshape(channels),
        grad_inv_rms.reshape(tokens),
    )


def solution(mesh):
    return jax.shard_map(
        local,
        mesh=mesh,
        in_specs=(
            P("ch", "ctx"),
            P("ch", "ctx"),
            P("ch"),
            P("ch", None),
            P("ch", None),
            P("ch", None),
            P("ch"),
        ),
        out_specs=(
            P("ch", "ctx"),
            P("ch"),
            P("ch", None),
            P("ch", None),
            P("ch", None),
            P("ch"),
            P("ctx"),
        ),
        check_vma=False,
    )
```
